256 devices in a mesh: seq: 64 (over z, y, core), head: 4 (over x).
Axes of the slice: x: 4, y: 4, z: 8, core: 2. Of those that a mesh axis runs over, the one named last changes fastest.
Arguments:
- queries: bfloat16 [16384, 4096], P('seq', 'head'), may hold values from -80 to 80, as said below
- keys_in: bfloat16 [16384, 4096], P('seq', 'head'), may hold values from -4 to 4
- values_in: bfloat16 [16384, 4096], P('seq', 'head'), may hold values from -6 to 6
- out_weight: bfloat16 [4096, 4096], P('head'), may hold values from -0.09375 to 0.09375
- spans: int32 [32], P('head'), may hold values from 1024 to 4096
- full_ids: int32 [8], P('head'), may hold values from 0 to 31, as said below
Outputs:
- mixed: bfloat16 [16384, 4096], P('seq', 'head')
The draws below stay inside these ranges and needn't reach their ends.
Inputs may be any that keep to these rules, and one draw needn't show every extreme that they name: `queries`: unlike a plain normal draw, some rows may be far larger than the rest. `full_ids`: increasing and distinct; entries g * 2 to (g + 1) * 2 - 1 name heads of group g, that is heads g * 8 to (g + 1) * 8 - 1.
All inputs are finite; a program needn't handle non-finite values.
Results may differ from the reference program's by a relative error of at most 0.012.
Values may be sent and summed in bfloat16 or wider, within the bound.
A program may use at most 128 MiB of HBM per device.

```python
import math
import jax
import jax.numpy as jnp
from jax import lax

HEADS = 32
FULL = 8
HEAD_DIM = 128
MODEL = 4096
SPAN_MAX = 4096
SPAN_MIN = 1024
SEQ = 16384
GROUP = 8
FULL_DEV = 2
N_HEAD = 4


def paired_draw(key):
    base_q = jnp.clip(jax.random.normal(jax.random.fold_in(key, 101), (SEQ, HEADS * HEAD_DIM), jnp.float32), -4.0, 4.0)
    base_k = jnp.clip(jax.random.normal(jax.random.fold_in(key, 202), (SEQ, HEADS * HEAD_DIM), jnp.float32), -4.0, 4.0)
    return (base_q, base_k)


def draw_queries(key, part):
    return paired_draw(key)[0].astype(jnp.bfloat16)


def draw_keys_in(key, part):
    return paired_draw(key)[1].astype(jnp.bfloat16)


def draw_full_ids(key, part):
    group_keys = jax.random.split(key, HEADS // GROUP)

    def pick_group(group_key):
        return jnp.sort(jax.random.permutation(group_key, GROUP)[:FULL_DEV])
    chosen = jax.vmap(pick_group)(group_keys)
    offsets = (jnp.arange(HEADS // GROUP) * GROUP)[:, None]
    return (chosen + offsets).reshape(FULL).astype(jnp.int32)


def touch_ends(values, rng, low, largest):
    dims = values.shape
    index_at = [jax.random.randint(jax.random.fold_in(rng, axis), (), 0, dims[axis]) for axis in range(len(dims))]
    values = values.at[tuple(index_at)].set(low)
    longest = dims.index(max(dims))
    index_at[longest] = (index_at[longest] + 1) % dims[longest]
    return values.at[tuple(index_at)].set(largest)


def shard_levels(rng, dims, pieces, smallest, largest):
    gain, own = 1.0, jax.random.fold_in(rng, 6)
    for axis_at, parts in pieces:
        steps = jnp.exp(jax.random.uniform(jax.random.fold_in(own, axis_at), (parts,), jnp.float32, smallest / len(pieces), largest / len(pieces)))
        gain = gain * jnp.repeat(steps, dims[axis_at] // parts).reshape([-1 if axis == axis_at else 1 for axis in range(len(dims))])
    return gain


def noise(stream_key, shape, spread, bound, cuts=(), kind=jnp.bfloat16):
    factor_of = shard_levels(stream_key, shape, cuts, -0.22, 0.18) if cuts else 1.0
    entries = jax.random.normal(stream_key, shape, jnp.float32) * spread * factor_of
    return jnp.minimum(jnp.maximum(entries, -bound), bound).astype(kind)


def setup_inputs(seed: int = 0) -> dict:
    key_list = jax.random.split(jax.random.key(seed), 7)
    return {
        "queries": draw_queries(jax.random.fold_in(key_list[6], 71), 0),
        "keys_in": draw_keys_in(jax.random.fold_in(key_list[6], 71), 0),
        "values_in": noise(key_list[2], (SEQ, HEADS * HEAD_DIM), 1.0, 6.0, ((0, 64), (1, 4))),
        "out_weight": noise(key_list[3], (HEADS * HEAD_DIM, MODEL), (HEADS * HEAD_DIM) ** -0.5, 0.09375, ((0, 4),)),
        "spans": touch_ends(jax.random.randint(key_list[4], (HEADS,), SPAN_MIN, SPAN_MAX + 1), jax.random.fold_in(key_list[4], 1), SPAN_MIN, SPAN_MAX).astype(jnp.int32),
        "full_ids": draw_full_ids(jax.random.fold_in(key_list[6], 71), 0),
    }


NEG_FILL = -1e30


def weigh(scores, allowed, value_rows):
    masked = jnp.where(allowed, scores, NEG_FILL)
    row_top = jnp.max(masked, axis=-1, keepdims=True)
    weights = jnp.where(allowed, jnp.exp(masked - row_top), 0.0)
    row_total = jnp.sum(weights, axis=-1, keepdims=True)
    rounded = lax.optimization_barrier(weights.astype(jnp.bfloat16)).astype(jnp.float32)
    numerator = jnp.dot(rounded, value_rows.astype(jnp.float32), precision=lax.Precision.HIGHEST)
    return numerator / row_total


def reference(queries, keys_in, values_in, out_weight, spans, full_ids):
    score_scale = HEAD_DIM ** -0.5
    block_rows = math.gcd(512, SEQ)
    block_starts = jnp.arange(SEQ // block_rows, dtype=jnp.int32) * block_rows
    positions = jnp.arange(SEQ, dtype=jnp.int32)
    head_range = jnp.arange(HEADS, dtype=jnp.int32)
    is_full = jnp.any(head_range[:, None] == full_ids[None, :], axis=1).astype(jnp.int32)
    ordering = jnp.argsort(is_full * HEADS + head_range).astype(jnp.int32)
    band_ids = ordering[: HEADS - FULL]
    full_list = ordering[HEADS - FULL:]

    def head_columns(array, head_id):
        return lax.dynamic_slice_in_dim(array, (head_id * HEAD_DIM).astype(jnp.int32), HEAD_DIM, 1)

    def banded_head(packed):
        head_id, reach = packed
        q_head = head_columns(queries, head_id).astype(jnp.float32)
        k_pad = jnp.pad(head_columns(keys_in, head_id).astype(jnp.float32), ((SPAN_MAX, 0), (0, 0)))
        v_pad = jnp.pad(head_columns(values_in, head_id).astype(jnp.float32), ((SPAN_MAX, 0), (0, 0)))

        def one_block(begin_row):
            q_rows = lax.dynamic_slice_in_dim(q_head, begin_row, block_rows, 0)
            k_rows = lax.dynamic_slice_in_dim(k_pad, begin_row, SPAN_MAX + block_rows, 0)
            v_rows = lax.dynamic_slice_in_dim(v_pad, begin_row, SPAN_MAX + block_rows, 0)
            scores = jnp.dot(q_rows, k_rows.T, precision=lax.Precision.HIGHEST) * score_scale
            q_pos = begin_row + jnp.arange(block_rows, dtype=jnp.int32)
            k_pos = begin_row - SPAN_MAX + jnp.arange(SPAN_MAX + block_rows, dtype=jnp.int32)
            gap_size = q_pos[:, None] - k_pos[None, :]
            allowed = (gap_size >= 0) & (gap_size < reach) & (k_pos >= 0)[None, :]
            return weigh(scores, allowed, v_rows)

        return lax.map(one_block, block_starts).reshape(SEQ, HEAD_DIM)

    def full_head(head_id):
        q_head = head_columns(queries, head_id).astype(jnp.float32)
        k_head = head_columns(keys_in, head_id).astype(jnp.float32)
        v_head = head_columns(values_in, head_id)

        def one_block(begin_row):
            q_rows = lax.dynamic_slice_in_dim(q_head, begin_row, block_rows, 0)
            scores = jnp.dot(q_rows, k_head.T, precision=lax.Precision.HIGHEST) * score_scale
            q_pos = begin_row + jnp.arange(block_rows, dtype=jnp.int32)
            allowed = positions[None, :] <= q_pos[:, None]
            return weigh(scores, allowed, v_head)

        return lax.map(one_block, block_starts).reshape(SEQ, HEAD_DIM)

    band_out = lax.map(banded_head, (band_ids, spans[band_ids]))
    full_out = lax.map(full_head, full_list)
    stacked = jnp.concatenate([band_out, full_out], axis=0).astype(jnp.bfloat16)
    inverse = jnp.argsort(ordering).astype(jnp.int32)
    per_head = jnp.take(stacked, inverse, axis=0)
    attended = per_head.transpose(1, 0, 2).reshape(SEQ, HEADS * HEAD_DIM)
    group_rows = HEADS * HEAD_DIM // N_HEAD
    summed = jnp.zeros((SEQ, MODEL), jnp.float32)
    for group_index in range(N_HEAD):
        lower = group_index * group_rows
        partial_value = jnp.dot(attended[:, lower:lower + group_rows], out_weight[lower:lower + group_rows], preferred_element_type=jnp.float32)
        summed = summed + lax.optimization_barrier(partial_value.astype(jnp.bfloat16)).astype(jnp.float32)
    return summed.astype(jnp.bfloat16)
```

```python
import functools
import math

import jax
import jax.numpy as jnp
from jax import lax
from jax.experimental import pallas as pl
from jax.experimental.pallas import tpu as pltpu
from jax.sharding import PartitionSpec as P

HD = 128
ROWS = 256
SCALE2 = HD ** (-0.5) * math.log2(math.e)
FILL = -1e30
FLOOR = -5e29
MESH = pl.DeviceIdType.MESH
ANY = pl.BlockSpec(memory_space=pl.ANY)
VM = pl.BlockSpec(memory_space=pltpu.VMEM)
BF = jnp.bfloat16
F32 = jnp.float32


def position():
    s = lax.axis_index("seq")
    return s, s // 8, (s // 2) % 4, s % 2, lax.axis_index("head")


def pick(slot, f0, f1):
    h = slot + (slot >= f0).astype(jnp.int32)
    h = h + (h >= f1).astype(jnp.int32)
    return jnp.where(slot == 6, f0, jnp.where(slot == 7, f1, h))


def local_full(full_ref):
    base = lax.axis_index("head") * 8
    return full_ref[0] - base, full_ref[1] - base


def arrange_body(ids, q, k, v, qh, kvh):
    qh[0] = q[...]
    kvh[0, 0] = k[...]
    kvh[0, 1] = v[...]


def arrange(local_ids, q, k, v):
    def column(i, ids):
        return (0, pick(i, ids[0], ids[1]))

    block = pl.BlockSpec((ROWS, HD), column)
    return pl.pallas_call(
        arrange_body,
        out_shape=(
            jax.ShapeDtypeStruct((8, ROWS, HD), BF),
            jax.ShapeDtypeStruct((8, 2, ROWS, HD), BF),
        ),
        grid_spec=pltpu.PrefetchScalarGridSpec(
            num_scalar_prefetch=1,
            grid=(8,),
            in_specs=[block, block, block],
            out_specs=[
                pl.BlockSpec((1, ROWS, HD), lambda i, ids: (i, 0, 0)),
                pl.BlockSpec((1, 2, ROWS, HD), lambda i, ids: (i, 0, 0, 0)),
            ],
        ),
        name="arrange",
    )(local_ids, q, k, v)


def greet(targets):
    barrier = pltpu.get_barrier_semaphore()
    for target in targets:
        pl.semaphore_signal(barrier, inc=1, device_id=target, device_id_type=MESH)
    pl.semaphore_wait(barrier, len(targets))


def plane_peers(s, hd):
    base = (s // 8) * 8
    return [(base + (s + r) % 8, hd) for r in range(1, 8)]


class Push:
    def __init__(self, src, dst, ssem, rsem, target, me, hd):
        self.remote = pltpu.make_async_remote_copy(
            src_ref=src, dst_ref=dst, send_sem=ssem, recv_sem=rsem, device_id=(target, hd), device_id_type=MESH
        )
        self.local = pltpu.make_async_copy(src, dst, rsem)
        self.away = target != me

    def start(self):
        @pl.when(self.away)
        def _():
            self.remote.start()

        @pl.when(jnp.logical_not(self.away))
        def _():
            self.local.start()

    def wait_send(self):
        @pl.when(self.away)
        def _():
            self.remote.wait_send()


def landed(ref, sem):
    pltpu.make_async_copy(ref, ref, sem).wait()


def exchange_body(
    qh, kvh, qb, kva, kvb, kvf, s_in, r_in, s_q, r_q, s_fa, r_fa, s_fb, r_fb, s_ff, r_ff, s_sa, r_sa, s_sb, r_sb, s_sf, r_sf
):
    s, z, y, c, hd = position()
    base = z * 8
    up, down = (s + 8) % 64, (s + 56) % 64
    sib = base + 2 * y + (1 - c)
    greet(plane_peers(s, hd) + [(up, hd), (down, hd)])

    sends = []

    def push(src, dst, ssem, rsem, target):
        one = Push(src, dst, ssem, rsem, target, s, hd)
        one.start()
        sends.append(one)

    half = y // 2
    for g in range(2):
        push(kvh.at[6 + g], kvf.at[z, c_of(y), y % 2], s_in.at[g], r_in.at[y % 2], base + 2 * (2 * g + c) + half)
    for t in range(4):
        push(kvh.at[t], kva.at[0, c, y], s_in.at[2 + t], r_in.at[2 + y], base + 2 * t + c)
    for g in range(2):
        push(kvh.at[4 + g], kvb.at[0, half, y % 2], s_in.at[6 + g], r_in.at[6 + y % 2], base + 2 * (2 * g + c) + half)
    place = 2 * (y % 2) + c
    for t in range(4):
        push(qh.at[t], qb.at[0, place], s_q.at[t], r_q.at[place], base + 2 * t + half)
        push(qh.at[4 + t // 2], qb.at[1, place], s_q.at[4 + t], r_q.at[4 + place], base + 2 * t + half)
        push(qh.at[6 + t // 2], qb.at[2, place], s_q.at[8 + t], r_q.at[8 + place], base + 2 * t + half)

    tails = []

    def ship(buf, ssem, rsem, target, cond=None):
        one = pltpu.make_async_remote_copy(
            src_ref=buf[0], dst_ref=buf[1], send_sem=ssem, recv_sem=rsem, device_id=(target, hd), device_id_type=MESH
        )
        if cond is None:
            one.start()
            tails.append((one, None))
        else:

            @pl.when(cond)
            def _():
                one.start()

            tails.append((one, cond))

    has_up = z < 7

    def hop_full(h):
        plane = (z + h) % 8
        mine = kvf.at[plane, c]
        if h == 0:
            for j in range(2):
                landed(kvf.at[plane, c, j], r_in.at[j])
        else:
            landed(mine, r_ff.at[h - 1])
        if h < 7:
            ship((mine, mine), s_ff.at[h], r_ff.at[h], down)
        if h == 0:
            ship((mine, mine), s_sf.at[h], r_sf.at[h], sib)
        else:
            ship((mine, mine), s_sf.at[h], r_sf.at[h], sib, plane < z)

    def hop_band(kv, n, first, s_f, r_f, s_s, r_s, d):
        mine = kv.at[d, c]
        if d == 0:
            for j in range(n):
                landed(kv.at[0, c, j], r_in.at[first + j])
            ship((mine, mine), s_s.at[0], r_s.at[0], sib)
            ship((mine, kv.at[1, c]), s_f.at[0], r_f.at[0], up, has_up)
        else:

            @pl.when(z >= d)
            def _():
                landed(mine, r_f.at[d - 1])

            ship((mine, mine), s_s.at[d], r_s.at[d], sib, z >= d)
            if d == 1:
                ship((mine, kv.at[2, c]), s_f.at[1], r_f.at[1], up, (z >= 1) & has_up)

    def band_a(d):
        hop_band(kva, 4, 2, s_fa, r_fa, s_sa, r_sa, d)

    def band_b(d):
        hop_band(kvb, 2, 6, s_fb, r_fb, s_sb, r_sb, d)

    hop_full(0)
    band_a(0)
    band_b(0)
    hop_full(1)
    hop_full(2)
    band_a(1)
    hop_full(3)
    band_b(1)
    hop_full(4)
    hop_full(5)
    band_a(2)
    hop_full(6)
    band_b(2)
    hop_full(7)

    for d in range(3):

        @pl.when(z >= d)
        def _():
            landed(kva.at[d, 1 - c], r_sa.at[d])
            landed(kvb.at[d, 1 - c], r_sb.at[d])

    for h in range(8):
        plane = (z + h) % 8

        @pl.when((plane < z) | (h == 0))
        def _():
            landed(kvf.at[plane, 1 - c], r_sf.at[h])

    for i in range(3):
        for j in range(4):
            landed(qb.at[i, j], r_q.at[4 * i + j])
    for one in sends:
        one.wait_send()
    for one, cond in tails:
        if cond is None:
            one.wait_send()
        else:

            @pl.when(cond)
            def _():
                one.wait_send()


def c_of(y):
    return y // 2


def exchange(qh, kvh):
    dma = pltpu.SemaphoreType.DMA
    counts = (8, 8, 12, 12, 2, 2, 2, 2, 7, 7, 3, 3, 3, 3, 8, 8)
    return pl.pallas_call(
        exchange_body,
        out_shape=(
            jax.ShapeDtypeStruct((3, 4, ROWS, HD), BF),
            jax.ShapeDtypeStruct((3, 2, 4, 2, ROWS, HD), BF),
            jax.ShapeDtypeStruct((3, 2, 2, 2, ROWS, HD), BF),
            jax.ShapeDtypeStruct((8, 2, 2, 2, ROWS, HD), BF),
        ),
        in_specs=[ANY, ANY],
        out_specs=(ANY, ANY, ANY, ANY),
        scratch_shapes=[dma((n,)) for n in counts],
        compiler_params=pltpu.CompilerParams(collective_id=0, has_side_effects=True),
        name="exchange",
    )(qh, kvh)


UNIT = 512


def attend_body(ids, spans, q, kva, kvb, kvf, o, lse, m_sc, l_sc, acc_sc):
    s, z, y, c, hd = position()
    pair, par = y // 2, y % 2
    here = 2 * z + c
    far = jnp.int32(1 << 20)

    def absorb(q_tile, k, v, q_first, k_first, reach):
        def scores():
            return SCALE2 * lax.dot_general(q_tile, k, (((1,), (1,)), ((), ())), preferred_element_type=F32)

        def update(sc):
            m_old = m_sc[...]
            m_new = jnp.maximum(m_old, jnp.max(sc, axis=1, keepdims=True))
            alpha = jnp.exp2(m_old - m_new)
            p = jnp.exp2(sc - jnp.tile(m_new, (1, UNIT // HD)))
            l_sc[...] = alpha * l_sc[...] + jnp.sum(p, axis=1, keepdims=True)
            acc_sc[...] = alpha * acc_sc[...] + jnp.dot(p.astype(BF), v, preferred_element_type=F32)
            m_sc[...] = m_new

        whole = (q_first >= k_first + 3 * ROWS - 1) & (q_first + ROWS - 1 - k_first < reach)

        @pl.when(whole)
        def _():
            update(scores())

        @pl.when(jnp.logical_not(whole))
        def _():
            row = lax.broadcasted_iota(jnp.int32, (ROWS, UNIT), 0)
            col = lax.broadcasted_iota(jnp.int32, (ROWS, UNIT), 1)
            gap = (q_first - k_first) + row - col - jnp.where(col >= ROWS, ROWS, 0)
            update(jnp.where((gap >= 0) & (gap < reach), scores(), FILL))

    def reset():
        m_sc[...] = jnp.full_like(m_sc, FLOOR)
        l_sc[...] = jnp.zeros_like(l_sc)
        acc_sc[...] = jnp.zeros_like(acc_sc)

    def store(t, which):
        l = l_sc[...]
        o[t, which] = (acc_sc[...] / jnp.where(l > 0.0, l, 1.0)).astype(BF)
        if which:
            total = jnp.where(l > 0.0, m_sc[...] + jnp.log2(jnp.where(l > 0.0, l, 1.0)), FILL)
            lse[t, which - 1] = total.T[:8]

    f0, f1 = ids[0], ids[1]
    reach_a = spans[pick(y, f0, f1)]
    reach_b = spans[pick(4 + pair, f0, f1)]

    def tile(t, _):
        q_first = (here * 4 + t) * ROWS

        def first_half(reach):
            return jnp.maximum(q_first - reach + 1, 0) // (4 * ROWS)

        reset()

        @pl.loop(2 * first_half(reach_a), 2 * here + 2)
        def _(n):
            hb, parity = n // 2, n % 2
            d, u = z - hb // 2, hb % 2
            absorb(
                q[0, t],
                kva[d, parity, pl.ds(2 * u, 2), 0].reshape(UNIT, HD),
                kva[d, parity, pl.ds(2 * u, 2), 1].reshape(UNIT, HD),
                q_first,
                hb * 4 * ROWS + parity * ROWS,
                reach_a,
            )

        store(t, 0)
        reset()

        @pl.loop(first_half(reach_b), here + 1)
        def _(hb):
            d, u = z - hb // 2, hb % 2
            absorb(
                q[1, t],
                kvb[d, u, :, 0].reshape(UNIT, HD),
                kvb[d, u, :, 1].reshape(UNIT, HD),
                q_first,
                hb * 4 * ROWS + par * ROWS,
                reach_b,
            )

        store(t, 1)
        reset()

        @pl.loop(0, here + 1)
        def _(hb):
            absorb(
                q[2, t],
                kvf[hb // 2, hb % 2, :, 0].reshape(UNIT, HD),
                kvf[hb // 2, hb % 2, :, 1].reshape(UNIT, HD),
                q_first,
                hb * 4 * ROWS + par * ROWS,
                far,
            )

        store(t, 2)
        return 0

    lax.fori_loop(0, 4, tile, 0)


def attend(local_ids, spans, qb, kva, kvb, kvf):
    return pl.pallas_call(
        attend_body,
        out_shape=(
            jax.ShapeDtypeStruct((4, 3, ROWS, HD), BF),
            jax.ShapeDtypeStruct((4, 2, 8, ROWS), F32),
        ),
        grid_spec=pltpu.PrefetchScalarGridSpec(
            num_scalar_prefetch=2,
            grid=(),
            in_specs=[VM] * 4,
            out_specs=[VM] * 2,
            scratch_shapes=[pltpu.VMEM((ROWS, HD), F32)] * 3,
        ),
        compiler_params=pltpu.CompilerParams(vmem_limit_bytes=40 << 20),
        name="attend",
    )(local_ids, spans, qb, kva, kvb, kvf)


def mix_body(ids, o, lse, w, out, wv, r, rl, merged, att, part, got, tmp, w_sem, s_o, r_o, s_l, r_l, s_x, r_x):
    s, z, y, c, hd = position()
    base = z * 8
    right, left = (hd + 1) % 4, (hd + 3) % 4
    pltpu.make_async_copy(w, wv, w_sem).start()
    greet(plane_peers(s, hd) + [(s, right), (s, left)])
    sends = []
    for t in range(4):
        home = base + 2 * (2 * c + t // 2) + t % 2
        for src, dst, ssem, rsem in ((o, r, s_o, r_o), (lse, rl, s_l, r_l)):
            one = Push(src.at[t], dst.at[y], ssem.at[t], rsem.at[y], home, s, hd)
            one.start()
            sends.append(one)
    for i in range(4):
        landed(r.at[i], r_o.at[i])
        landed(rl.at[i], r_l.at[i])
    for i in range(4):
        merged[i] = r[i, 0]
    for which in range(2):
        for pair in range(2):
            one, two = 2 * pair, 2 * pair + 1

            def column(i):
                return jnp.tile(rl[i, which], (16, 1)).T

            a, b = column(one), column(two)
            top = jnp.maximum(a, b)
            wa, wb = jnp.exp2(a - top), jnp.exp2(b - top)
            value = wa * r[one, which + 1].astype(F32) + wb * r[two, which + 1].astype(F32)
            merged[4 + 2 * which + pair] = (value / (wa + wb)).astype(BF)
    f0, f1 = ids[0], ids[1]
    for h in range(8):
        band = h - jnp.where(h > f0, 1, 0) - jnp.where(h > f1, 1, 0)
        slot = jnp.where(f0 == h, 6, jnp.where(f1 == h, 7, jnp.clip(band, 0, 5)))
        att[:, h * HD : (h + 1) * HD] = merged[slot]
    for one in sends:
        one.wait_send()
    landed(wv, w_sem)

    def project(dest):
        for half in range(2):
            for sub in range(2):
                columns = pl.ds(pl.multiple_of(dest * 1024 + half * 512 + sub * 256, 256), 256)
                piece = jnp.dot(att[...], wv[:, columns], preferred_element_type=F32)
                part[dest, half, :, sub * 256 : (sub + 1) * 256] = piece.astype(BF)

    def ship(src, slot, target):
        one = pltpu.make_async_remote_copy(
            src_ref=src,
            dst_ref=got.at[slot],
            send_sem=s_x.at[slot],
            recv_sem=r_x.at[slot],
            device_id=(s, target),
            device_id_type=MESH,
        )
        one.start()
        return one

    across = (hd + 2) % 4
    project(across)
    moved = [ship(part.at[across, 0], 0, right), ship(part.at[across, 1], 1, left)]
    project(right)
    moved.append(ship(part.at[right, 1], 2, right))
    project(left)
    moved.append(ship(part.at[left, 0], 3, left))
    landed(got.at[0], r_x.at[0])
    tmp[0] = (got[0].astype(F32) + part[right, 0].astype(F32)).astype(BF)
    moved.append(ship(tmp.at[0], 4, right))
    landed(got.at[1], r_x.at[1])
    tmp[1] = (got[1].astype(F32) + part[left, 1].astype(F32)).astype(BF)
    moved.append(ship(tmp.at[1], 5, left))
    project(hd)
    landed(got.at[2], r_x.at[2])
    landed(got.at[3], r_x.at[3])
    landed(got.at[4], r_x.at[4])
    out[:, :512] = (part[hd, 0].astype(F32) + got[4].astype(F32) + got[3].astype(F32)).astype(BF)
    landed(got.at[5], r_x.at[5])
    out[:, 512:] = (part[hd, 1].astype(F32) + got[5].astype(F32) + got[2].astype(F32)).astype(BF)
    for one in moved:
        one.wait_send()


def mix(local_ids, o, lse, w):
    dma = pltpu.SemaphoreType.DMA
    return pl.pallas_call(
        mix_body,
        out_shape=jax.ShapeDtypeStruct((ROWS, 1024), BF),
        in_specs=[pl.BlockSpec(memory_space=pltpu.SMEM), ANY, ANY, ANY],
        out_specs=VM,
        scratch_shapes=[
            pltpu.VMEM((1024, 4096), BF),
            pltpu.VMEM((4, 3, ROWS, HD), BF),
            pltpu.VMEM((4, 2, 8, ROWS), F32),
            pltpu.VMEM((8, ROWS, HD), BF),
            pltpu.VMEM((ROWS, 1024), BF),
            pltpu.VMEM((4, 2, ROWS, 512), BF),
            pltpu.VMEM((6, ROWS, 512), BF),
            pltpu.VMEM((2, ROWS, 512), BF),
            dma(()),
            dma((4,)),
            dma((4,)),
            dma((4,)),
            dma((4,)),
            dma((6,)),
            dma((6,)),
        ],
        compiler_params=pltpu.CompilerParams(collective_id=1, has_side_effects=True, vmem_limit_bytes=40 << 20),
        name="mix",
    )(local_ids, o, lse, w)


def on_device(queries, keys_in, values_in, out_weight, spans, full_ids):
    local_ids = full_ids - lax.axis_index("head") * 8
    qh, kvh = arrange(local_ids, queries, keys_in, values_in)
    qb, kva, kvb, kvf = exchange(qh, kvh)
    o, lse = attend(local_ids, spans, qb, kva, kvb, kvf)
    return mix(local_ids, o, lse, out_weight)


def solution(mesh):
    placed = (P("seq", "head"), P("seq", "head"), P("seq", "head"), P("head", None), P("head"), P("head"))
    return jax.shard_map(on_device, mesh=mesh, in_specs=placed, out_specs=P("seq", "head"), check_vma=False)
```

```python
import functools
import math

import jax
import jax.numpy as jnp
from jax import lax
from jax.experimental import pallas as pl
from jax.experimental.pallas import tpu as pltpu
from jax.sharding import PartitionSpec as P

HD = 128
ROWS = 256
SCALE2 = HD ** (-0.5) * math.log2(math.e)
FILL = -1e30
FLOOR = -5e29
MESH = pl.DeviceIdType.MESH
ANY = pl.BlockSpec(memory_space=pl.ANY)
VM = pl.BlockSpec(memory_space=pltpu.VMEM)
BF = jnp.bfloat16
F32 = jnp.float32


def position():
    s = lax.axis_index("seq")
    return s, s // 8, (s // 2) % 4, s % 2, lax.axis_index("head")


def pick(slot, f0, f1):
    h = slot + (slot >= f0).astype(jnp.int32)
    h = h + (h >= f1).astype(jnp.int32)
    return jnp.where(slot == 6, f0, jnp.where(slot == 7, f1, h))


def arrange_body(ids, q, k, v, qh, kvh):
    base = lax.axis_index("head") * 8
    f0, f1 = ids[0] - base, ids[1] - base
    for i in range(8):
        h = jnp.clip(pick(jnp.int32(i), f0, f1), 0, 7)
        columns = pl.ds(pl.multiple_of(h * HD, HD), HD)
        qh[i] = q[:, columns]
        kvh[i, 0] = k[:, columns]
        kvh[i, 1] = v[:, columns]


def arrange(full_ids, q, k, v):
    return pl.pallas_call(
        arrange_body,
        out_shape=(
            jax.ShapeDtypeStruct((8, ROWS, HD), BF),
            jax.ShapeDtypeStruct((8, 2, ROWS, HD), BF),
        ),
        in_specs=[pl.BlockSpec(memory_space=pltpu.SMEM), VM, VM, VM],
        out_specs=[VM, VM],
        name="arrange",
    )(full_ids, q, k, v)


def greet(targets):
    barrier = pltpu.get_barrier_semaphore()
    for target in targets:
        pl.semaphore_signal(barrier, inc=1, device_id=target, device_id_type=MESH)
    pl.semaphore_wait(barrier, len(targets))


def plane_peers(s, hd):
    base = (s // 8) * 8
    return [(base + (s + r) % 8, hd) for r in range(1, 8)]


class Push:
    def __init__(self, src, dst, ssem, rsem, target, me, hd):
        self.remote = pltpu.make_async_remote_copy(
            src_ref=src, dst_ref=dst, send_sem=ssem, recv_sem=rsem, device_id=(target, hd), device_id_type=MESH
        )
        self.local = pltpu.make_async_copy(src, dst, rsem)
        self.away = target != me

    def start(self):
        @pl.when(self.away)
        def _():
            self.remote.start()

        @pl.when(jnp.logical_not(self.away))
        def _():
            self.local.start()

    def wait_send(self):
        @pl.when(self.away)
        def _():
            self.remote.wait_send()


def landed(ref, sem):
    pltpu.make_async_copy(ref, ref, sem).wait()


TASKS = (
    (0, 0, 0),
    (0, 0, 1),
    (2, 0, 0),
    (1, 0, 0),
    (2, 1, 0),
    (0, 1, 0),
    (2, 2, 0),
    (0, 1, 1),
    (2, 3, 0),
    (1, 1, 0),
    (2, 4, 0),
    (0, 2, 0),
    (2, 5, 0),
    (0, 2, 1),
    (2, 6, 0),
    (1, 2, 0),
    (2, 7, 0),
)
MOVES = {
    1: (("f", 1),),
    2: (("b", 0), ("f", 2)),
    4: (("a", 1), ("f", 3)),
    6: (("f", 4),),
    8: (("b", 1), ("f", 5)),
    10: (("f", 6), ("a", 2)),
    12: (("f", 7),),
    13: (("b", 2),),
}


def table(n, values):
    out = jnp.int32(values[0])
    for i, value in enumerate(values[1:], 1):
        out = jnp.where(n == i, value, out)
    return out


def whole_body(
    ids, spans, qh, kvh, w, out,
    wv, kv, qb, o, lse, r, rl, merged, att, part, got, tmp, m_sc, l_sc, acc_sc, rel,
    w_sem, s_in, r_in, s_q, r_q, s_fa, r_fa, s_fb, r_fb, s_ff, r_ff, s_sa, r_sa, s_sb, r_sb, s_sf, r_sf,
    s_o, r_o, s_l, r_l, s_x, r_x,
):
    s, z, y, c, hd = position()
    pair, par = y // 2, y % 2
    base = z * 8
    up, down = (s + 8) % 64, (s + 56) % 64
    sib = base + 2 * y + (1 - c)
    right, left = (hd + 1) % 4, (hd + 3) % 4
    half = y // 2
    pltpu.make_async_copy(w, wv, w_sem).start()
    greet(plane_peers(s, hd) + [(up, hd), (down, hd), (s, right), (s, left)])

    sends = []

    def push(src, dst, ssem, rsem, target):
        one = Push(src, dst, ssem, rsem, target, s, hd)
        one.start()
        sends.append(one)

    def push_q(i, slot):
        for t in range(4):
            push(qh.at[slot(t)], qb.at[i, place], s_q.at[4 * i + t], r_q.at[4 * i + place], base + 2 * t + half)

    place = 2 * (y % 2) + c
    for g in range(2):
        push(kvh.at[6 + g], kv.at[9 + z, y], s_in.at[g], r_in.at[y % 2], base + 2 * (2 * g + c) + half)
    for t in range(4):
        push(kvh.at[t], kv.at[c, y], s_in.at[2 + t], r_in.at[2 + y], base + 2 * t + c)
    push_q(0, lambda t: t)
    push_q(2, lambda t: 6 + t // 2)
    for g in range(2):
        push(kvh.at[4 + g], kv.at[6, y], s_in.at[6 + g], r_in.at[6 + y % 2], base + 2 * (2 * g + c) + half)
    push_q(1, lambda t: 4 + t // 2)

    row = lax.broadcasted_iota(jnp.int32, (ROWS, 4 * ROWS), 0)
    col = lax.broadcasted_iota(jnp.int32, (ROWS, 4 * ROWS), 1)
    rel[...] = row - col - (col // ROWS) * ROWS
    m_sc[...] = jnp.full_like(m_sc, FLOOR)
    l_sc[...] = jnp.zeros_like(l_sc)
    acc_sc[...] = jnp.zeros_like(acc_sc)

    def hop(src, dst, ssem, rsem, target):
        return pltpu.make_async_remote_copy(
            src_ref=src, dst_ref=dst, send_sem=ssem, recv_sem=rsem, device_id=(target, hd), device_id_type=MESH
        )

    def when(cond, action):
        pl.when(cond)(action)

    mine2 = pl.ds(2 * c, 2)
    other2 = pl.ds(2 * (1 - c), 2)

    def full_down(h):
        ref = kv.at[9 + (z + h) % 8, mine2]
        return hop(ref, ref, s_ff.at[h], r_ff.at[h], down)

    def full_sib(h):
        ref = kv.at[9 + (z + h) % 8, mine2]
        return hop(ref, ref, s_sf.at[h], r_sf.at[h], sib)

    def needed(h):
        return z + h > 7 if h else z >= 0

    def move_full(h):
        if h == 0:
            for j in range(2):
                landed(kv.at[9 + z, 2 * c + j], r_in.at[j])
        else:
            landed(kv.at[9 + (z + h) % 8, mine2], r_ff.at[h - 1])
        if h < 7:
            full_down(h).start()
        when(needed(h), full_sib(h).start)

    def band_up(kind, d):
        if kind == "a":
            return hop(kv.at[2 * d + c], kv.at[2 * d + 2 + c], s_fa.at[d], r_fa.at[d], up)
        return hop(kv.at[6 + d, mine2], kv.at[7 + d, mine2], s_fb.at[d], r_fb.at[d], up)

    def band_sib(kind, d):
        if kind == "a":
            return hop(kv.at[2 * d + c], kv.at[2 * d + c], s_sa.at[d], r_sa.at[d], sib)
        return hop(kv.at[6 + d, mine2], kv.at[6 + d, mine2], s_sb.at[d], r_sb.at[d], sib)

    def move_band(kind, d):
        if d == 0 and kind == "a":
            for j in range(4):
                landed(kv.at[c, j], r_in.at[2 + j])
        elif d == 0:
            for j in range(2):
                landed(kv.at[6, 2 * c + j], r_in.at[6 + j])
        else:

            @pl.when(z >= d)
            def _():
                if kind == "a":
                    landed(kv.at[2 * d + c], r_fa.at[d - 1])
                else:
                    landed(kv.at[6 + d, mine2], r_fb.at[d - 1])

        if d < 2:
            when((z >= d) & (z < 7), band_up(kind, d).start)
        when(z >= d, band_sib(kind, d).start)

    move_full(0)
    move_band("a", 0)

    f0, f1 = ids[0] - hd * 8, ids[1] - hd * 8
    reach_a = spans[jnp.clip(pick(y, f0, f1), 0, 7)]
    reach_b = spans[jnp.clip(pick(4 + pair, f0, f1), 0, 7)]
    q_start = base * ROWS + c * 4 * ROWS

    def absorb(which, chunk, first, units, off, reach, masked):
        keys = units * ROWS
        k = kv[chunk, pl.ds(first, units), 0].reshape(keys, HD)
        v = kv[chunk, pl.ds(first, units), 1].reshape(keys, HD)

        def scores(t):
            sc = SCALE2 * lax.dot_general(
                qb[which, t], k, (((1,), (1,)), ((), ())), preferred_element_type=F32
            )
            if masked:
                at = rel[:, :keys]
                low = -(off + t * ROWS)
                sc = jnp.where((at >= low) & (at < low + reach), sc, FILL)
            return sc

        def soft(t, sc):
            m_old = m_sc[which, t]
            m_new = jnp.maximum(m_old, jnp.max(sc, axis=1, keepdims=True))
            alpha = jnp.exp2(m_old - m_new)
            p = jnp.exp2(sc - jnp.tile(m_new, (1, keys // HD)))
            m_sc[which, t] = m_new
            l_sc[which, t] = alpha * l_sc[which, t] + jnp.sum(p, axis=1, keepdims=True)
            return p.astype(BF), alpha

        def gather(t, p, alpha):
            acc_sc[which, t] = alpha * acc_sc[which, t] + jnp.dot(p, v, preferred_element_type=F32)

        current, pending = scores(0), None
        for t in range(4):
            following = scores(t + 1) if t < 3 else None
            weights = soft(t, current)
            if pending is not None:
                gather(*pending)
            pending = (t, *weights)
            current = following
        gather(*pending)

    def step(n, _):
        for at, moves in MOVES.items():

            @pl.when(n == at)
            def _(moves=moves):
                for kind, d in moves:
                    if kind == "f":
                        move_full(d)
                    else:
                        move_band(kind, d)

        for at, (which, d, other) in enumerate(TASKS):

            @pl.when(n == at)
            def _(which=which, d=d, other=other):
                if d == 0 and not other:
                    for j in range(4):
                        landed(qb.at[which, j], r_q.at[4 * which + j])
                if which == 0 and other:
                    when(z >= d, lambda: landed(kv.at[2 * d + 1 - c], r_sa.at[d]))
                if which == 1:
                    when(z >= d, lambda: landed(kv.at[6 + d, other2], r_sb.at[d]))
                if which == 2:
                    when(needed(d), lambda: landed(kv.at[9 + (z + d) % 8, other2], r_sf.at[d]))

        which = table(n, [t[0] for t in TASKS])
        d = table(n, [t[1] for t in TASKS])
        other = table(n, [t[2] for t in TASKS])
        side = jnp.where(other == 1, 1 - c, c)
        full = which == 2
        plane = jnp.where(full, (z + d) % 8, z - d)
        chunk = jnp.where(full, 9 + plane, jnp.where(which == 1, 6 + d, 2 * d + side))
        valid = jnp.where(full, (d == 0) | (plane < z), z >= d)
        parity = jnp.where(which == 0, side, par)
        off = q_start - plane * 8 * ROWS - parity * ROWS
        reach = jnp.where(full, 1 << 20, jnp.where(which == 1, reach_b, reach_a))
        lower = (d == 0) & (c == 0)
        upper = jnp.logical_not(full) & (d == 2) & (c == 1)
        plain = full & (d > 0)

        @pl.when(valid & plain)
        def _():
            absorb(which, chunk, 0, 4, off, reach, False)

        @pl.when(valid & jnp.logical_not(plain | lower | upper))
        def _():
            absorb(which, chunk, 0, 4, off, reach, True)

        @pl.when(valid & (lower | upper))
        def _():
            first = jnp.where(upper, 2, 0)
            absorb(which, chunk, first, 2, off - first * 2 * ROWS, reach, True)

        return 0

    lax.fori_loop(0, len(TASKS), step, 0)

    def send_back(t, _):
        for which in range(3):
            total = l_sc[which, t]
            safe = jnp.where(total > 0.0, total, 1.0)
            o[t, which] = (acc_sc[which, t] / safe).astype(BF)
            if which:
                level = jnp.where(total > 0.0, m_sc[which, t] + jnp.log2(safe), FILL)
                lse[t, which - 1] = level.T[:8]
        for back in backs(t):
            back.start()
        return 0

    def backs(t):
        home = base + 2 * (2 * c + t // 2) + t % 2
        return [
            Push(o.at[t], r.at[y], s_o.at[t], r_o.at[y], home, s, hd),
            Push(lse.at[t], rl.at[y], s_l.at[t], r_l.at[y], home, s, hd),
        ]

    lax.fori_loop(0, 4, send_back, 0)
    for i in range(4):
        landed(r.at[i], r_o.at[i])
        landed(rl.at[i], r_l.at[i])
    for i in range(4):
        merged[i] = r[i, 0]
    for which in range(2):
        for two in range(2):
            first, second = 2 * two, 2 * two + 1

            def column(i):
                return jnp.tile(rl[i, which], (16, 1)).T

            a, b = column(first), column(second)
            top = jnp.maximum(a, b)
            wa, wb = jnp.exp2(a - top), jnp.exp2(b - top)
            value = wa * r[first, which + 1].astype(F32) + wb * r[second, which + 1].astype(F32)
            merged[4 + 2 * which + two] = (value / (wa + wb)).astype(BF)
    for h in range(8):
        band = h - jnp.where(h > f0, 1, 0) - jnp.where(h > f1, 1, 0)
        slot = jnp.where(f0 == h, 6, jnp.where(f1 == h, 7, jnp.clip(band, 0, 5)))
        att[:, h * HD : (h + 1) * HD] = merged[slot]
    landed(wv, w_sem)

    def project(dest):
        for side in range(2):
            for sub in range(2):
                columns = pl.ds(pl.multiple_of(dest * 1024 + side * 512 + sub * 256, 256), 256)
                piece = jnp.dot(att[...], wv[:, columns], preferred_element_type=F32)
                part[dest, side, :, sub * 256 : (sub + 1) * 256] = piece.astype(BF)

    def ship(src, slot, target):
        one = pltpu.make_async_remote_copy(
            src_ref=src,
            dst_ref=got.at[slot],
            send_sem=s_x.at[slot],
            recv_sem=r_x.at[slot],
            device_id=(s, target),
            device_id_type=MESH,
        )
        one.start()
        return one

    across = (hd + 2) % 4
    project(across)
    moved = [ship(part.at[across, 0], 0, right), ship(part.at[across, 1], 1, left)]
    project(right)
    moved.append(ship(part.at[right, 1], 2, right))
    project(left)
    moved.append(ship(part.at[left, 0], 3, left))
    landed(got.at[0], r_x.at[0])
    tmp[0] = (got[0].astype(F32) + part[right, 0].astype(F32)).astype(BF)
    moved.append(ship(tmp.at[0], 4, right))
    landed(got.at[1], r_x.at[1])
    tmp[1] = (got[1].astype(F32) + part[left, 1].astype(F32)).astype(BF)
    moved.append(ship(tmp.at[1], 5, left))
    project(hd)
    for one in sends:
        one.wait_send()
    for h in range(7):
        full_down(h).wait_send()
    for h in range(8):
        when(needed(h), full_sib(h).wait_send)
    for kind in ("a", "b"):
        for d in range(3):
            if d < 2:
                when((z >= d) & (z < 7), band_up(kind, d).wait_send)
            when(z >= d, band_sib(kind, d).wait_send)
    for t in range(4):
        for back in backs(t):
            back.wait_send()
    landed(got.at[2], r_x.at[2])
    landed(got.at[3], r_x.at[3])
    landed(got.at[4], r_x.at[4])
    out[:, :512] = (part[hd, 0].astype(F32) + got[4].astype(F32) + got[3].astype(F32)).astype(BF)
    landed(got.at[5], r_x.at[5])
    out[:, 512:] = (part[hd, 1].astype(F32) + got[5].astype(F32) + got[2].astype(F32)).astype(BF)
    for one in moved:
        one.wait_send()


def whole(full_ids, spans, qh, kvh, w):
    dma = pltpu.SemaphoreType.DMA
    counts = (8, 8, 12, 12, 2, 2, 2, 2, 7, 7, 3, 3, 3, 3, 8, 8, 4, 4, 4, 4, 6, 6)
    smem = pl.BlockSpec(memory_space=pltpu.SMEM)
    return pl.pallas_call(
        whole_body,
        out_shape=jax.ShapeDtypeStruct((ROWS, 1024), BF),
        in_specs=[smem, smem, ANY, ANY, ANY],
        out_specs=VM,
        scratch_shapes=[
            pltpu.VMEM((1024, 4096), BF),
            pltpu.VMEM((17, 4, 2, ROWS, HD), BF),
            pltpu.VMEM((3, 4, ROWS, HD), BF),
            pltpu.VMEM((4, 3, ROWS, HD), BF),
            pltpu.VMEM((4, 2, 8, ROWS), F32),
            pltpu.VMEM((4, 3, ROWS, HD), BF),
            pltpu.VMEM((4, 2, 8, ROWS), F32),
            pltpu.VMEM((8, ROWS, HD), BF),
            pltpu.VMEM((ROWS, 1024), BF),
            pltpu.VMEM((4, 2, ROWS, 512), BF),
            pltpu.VMEM((6, ROWS, 512), BF),
            pltpu.VMEM((2, ROWS, 512), BF),
            pltpu.VMEM((3, 4, ROWS, HD), F32),
            pltpu.VMEM((3, 4, ROWS, HD), F32),
            pltpu.VMEM((3, 4, ROWS, HD), F32),
            pltpu.VMEM((ROWS, 4 * ROWS), jnp.int32),
            dma(()),
        ]
        + [dma((n,)) for n in counts],
        compiler_params=pltpu.CompilerParams(collective_id=0, has_side_effects=True, vmem_limit_bytes=56 << 20),
        name="whole",
    )(full_ids, spans, qh, kvh, w)


def on_device(queries, keys_in, values_in, out_weight, spans, full_ids):
    qh, kvh = arrange(full_ids, queries, keys_in, values_in)
    return whole(full_ids, spans, qh, kvh, out_weight)


def solution(mesh):
    placed = (P("seq", "head"), P("seq", "head"), P("seq", "head"), P("head", None), P("head"), P("head"))
    return jax.shard_map(on_device, mesh=mesh, in_specs=placed, out_specs=P("seq", "head"), check_vma=False)
```

```python
import functools
import math

import jax
import jax.numpy as jnp
from jax import lax
from jax.experimental import pallas as pl
from jax.experimental.pallas import tpu as pltpu
from jax.sharding import PartitionSpec as P

HD = 128
ROWS = 256
SCALE2 = HD ** (-0.5) * math.log2(math.e)
FILL = -1e30
FLOOR = -5e29
MESH = pl.DeviceIdType.MESH
ANY = pl.BlockSpec(memory_space=pl.ANY)
VM = pl.BlockSpec(memory_space=pltpu.VMEM)
BF = jnp.bfloat16
F32 = jnp.float32


def position():
    s = lax.axis_index("seq")
    return s, s // 8, (s // 2) % 4, s % 2, lax.axis_index("head")


def pick(slot, f0, f1):
    h = slot + (slot >= f0).astype(jnp.int32)
    h = h + (h >= f1).astype(jnp.int32)
    return jnp.where(slot == 6, f0, jnp.where(slot == 7, f1, h))


def arrange_body(ids, q, k, v, qh, kvh):
    base = lax.axis_index("head") * 8
    f0, f1 = ids[0] - base, ids[1] - base
    for i in range(8):
        h = jnp.clip(pick(jnp.int32(i), f0, f1), 0, 7)
        columns = pl.ds(pl.multiple_of(h * HD, HD), HD)
        qh[i] = q[:, columns]
        kvh[i, 0] = k[:, columns]
        kvh[i, 1] = v[:, columns]


def arrange(full_ids, q, k, v):
    return pl.pallas_call(
        arrange_body,
        out_shape=(
            jax.ShapeDtypeStruct((8, ROWS, HD), BF),
            jax.ShapeDtypeStruct((8, 2, ROWS, HD), BF),
        ),
        in_specs=[pl.BlockSpec(memory_space=pltpu.SMEM), VM, VM, VM],
        out_specs=[VM, VM],
        name="arrange",
    )(full_ids, q, k, v)


def greet(targets):
    barrier = pltpu.get_barrier_semaphore()
    for target in targets:
        pl.semaphore_signal(barrier, inc=1, device_id=target, device_id_type=MESH)
    pl.semaphore_wait(barrier, len(targets))


def plane_peers(s, hd):
    base = (s // 8) * 8
    return [(base + (s + r) % 8, hd) for r in range(1, 8)]


class Push:
    def __init__(self, src, dst, ssem, rsem, target, me, hd):
        self.remote = pltpu.make_async_remote_copy(
            src_ref=src, dst_ref=dst, send_sem=ssem, recv_sem=rsem, device_id=(target, hd), device_id_type=MESH
        )
        self.local = pltpu.make_async_copy(src, dst, rsem)
        self.away = target != me

    def start(self):
        @pl.when(self.away)
        def _():
            self.remote.start()

        @pl.when(jnp.logical_not(self.away))
        def _():
            self.local.start()

    def wait_send(self):
        @pl.when(self.away)
        def _():
            self.remote.wait_send()


def landed(ref, sem):
    pltpu.make_async_copy(ref, ref, sem).wait()


TASKS = (
    (0, 0, 0),
    (0, 0, 1),
    (2, 0, 0),
    (2, 1, 0),
    (1, 0, 0),
    (2, 2, 0),
    (0, 1, 0),
    (2, 3, 0),
    (0, 1, 1),
    (2, 4, 0),
    (1, 1, 0),
    (2, 5, 0),
    (0, 2, 0),
    (2, 6, 0),
    (0, 2, 1),
    (1, 2, 0),
    (2, 7, 0),
)
MOVES = {3: (("b", 0),), 4: (("a", 1),), 8: (("b", 1),), 11: (("a", 2),), 14: (("b", 2),)}


def table(n, values):
    out = jnp.int32(values[0])
    for i, value in enumerate(values[1:], 1):
        out = jnp.where(n == i, value, out)
    return out


def whole_body(
    ids, spans, qh, kvh, w, out,
    wv, kv, qb, o, lse, r, rl, merged, att, part, got, tmp, m_sc, l_sc, acc_sc, rel,
    w_sem, s_in, r_in, s_q, r_q, s_fa, r_fa, s_fb, r_fb, s_ff, r_ff, s_sa, r_sa, s_sb, r_sb, s_sf, r_sf,
    s_o, r_o, s_l, r_l, s_x, r_x,
):
    s, z, y, c, hd = position()
    pair, par = y // 2, y % 2
    base = z * 8
    up, down = (s + 8) % 64, (s + 56) % 64
    sib = base + 2 * y + (1 - c)
    right, left = (hd + 1) % 4, (hd + 3) % 4
    half = y // 2
    pltpu.make_async_copy(w, wv, w_sem).start()
    greet(plane_peers(s, hd) + [(up, hd), (down, hd), (s, right), (s, left)])

    sends = []

    def push(src, dst, ssem, rsem, target):
        one = Push(src, dst, ssem, rsem, target, s, hd)
        one.start()
        sends.append(one)

    def push_q(i, slot):
        for t in range(4):
            push(qh.at[slot(t)], qb.at[i, place], s_q.at[4 * i + t], r_q.at[4 * i + place], base + 2 * t + half)

    place = 2 * (y % 2) + c
    def prepare():
        row = lax.broadcasted_iota(jnp.int32, (ROWS, 4 * ROWS), 0)
        col = lax.broadcasted_iota(jnp.int32, (ROWS, 4 * ROWS), 1)
        rel[...] = row - col - (col // ROWS) * ROWS
        m_sc[...] = jnp.full_like(m_sc, FLOOR)
        l_sc[...] = jnp.zeros_like(l_sc)
        acc_sc[...] = jnp.zeros_like(acc_sc)

    def hop(src, dst, ssem, rsem, target):
        return pltpu.make_async_remote_copy(
            src_ref=src, dst_ref=dst, send_sem=ssem, recv_sem=rsem, device_id=(target, hd), device_id_type=MESH
        )

    def when(cond, action):
        pl.when(cond)(action)

    mine2 = pl.ds(2 * c, 2)
    other2 = pl.ds(2 * (1 - c), 2)

    def full_down(h, j):
        ref = kv.at[9 + (z + h) % 8, 2 * c + j]
        return hop(ref, ref, s_ff.at[2 * h + j], r_ff.at[2 * h + j], down)

    def full_sib(h):
        ref = kv.at[9 + (z + h) % 8, mine2]
        return hop(ref, ref, s_sf.at[h], r_sf.at[h], sib)

    def needed(h):
        return z + h > 7 if h else z >= 0

    def move_full(h, j):
        ref = kv.at[9 + (z + h) % 8, 2 * c + j]
        landed(ref, r_in.at[j] if h == 0 else r_ff.at[2 * h - 2 + j])
        if h < 7:
            full_down(h, j).start()
        if j == 1:
            when(needed(h), full_sib(h).start)

    def band_up(kind, d):
        if kind == "a":
            return hop(kv.at[2 * d + c], kv.at[2 * d + 2 + c], s_fa.at[d], r_fa.at[d], up)
        return hop(kv.at[6 + d, mine2], kv.at[7 + d, mine2], s_fb.at[d], r_fb.at[d], up)

    def band_sib(kind, d):
        if kind == "a":
            return hop(kv.at[2 * d + c], kv.at[2 * d + c], s_sa.at[d], r_sa.at[d], sib)
        return hop(kv.at[6 + d, mine2], kv.at[6 + d, mine2], s_sb.at[d], r_sb.at[d], sib)

    def move_band(kind, d):
        if d == 0 and kind == "a":
            for j in range(4):
                landed(kv.at[c, j], r_in.at[2 + j])
        elif d == 0:
            for j in range(2):
                landed(kv.at[6, 2 * c + j], r_in.at[6 + j])
        else:

            @pl.when(z >= d)
            def _():
                if kind == "a":
                    landed(kv.at[2 * d + c], r_fa.at[d - 1])
                else:
                    landed(kv.at[6 + d, mine2], r_fb.at[d - 1])

        if d < 2:
            when((z >= d) & (z < 7), band_up(kind, d).start)
        when(z >= d, band_sib(kind, d).start)

    for g in range(2):
        push(kvh.at[6 + g], kv.at[9 + z, y], s_in.at[g], r_in.at[y % 2], base + 2 * (2 * g + c) + half)
    prepare()
    move_full(0, 0)
    move_full(0, 1)
    for t in range(4):
        push(kvh.at[t], kv.at[c, y], s_in.at[2 + t], r_in.at[2 + y], base + 2 * t + c)
    push_q(0, lambda t: t)
    move_full(1, 0)
    move_band("a", 0)
    push_q(2, lambda t: 6 + t // 2)
    for g in range(2):
        push(kvh.at[4 + g], kv.at[6, y], s_in.at[6 + g], r_in.at[6 + y % 2], base + 2 * (2 * g + c) + half)
    move_full(1, 1)
    move_full(2, 0)
    push_q(1, lambda t: 4 + t // 2)

    f0, f1 = ids[0] - hd * 8, ids[1] - hd * 8
    reach_a = spans[jnp.clip(pick(y, f0, f1), 0, 7)]
    reach_b = spans[jnp.clip(pick(4 + pair, f0, f1), 0, 7)]
    q_start = base * ROWS + c * 4 * ROWS

    def absorb(which, chunk, first, units, off, reach, masked):
        keys = units * ROWS
        k = kv[chunk, pl.ds(first, units), 0].reshape(keys, HD)
        v = kv[chunk, pl.ds(first, units), 1].reshape(keys, HD)

        def scores(t):
            sc = SCALE2 * lax.dot_general(
                qb[which, t], k, (((1,), (1,)), ((), ())), preferred_element_type=F32
            )
            if masked:
                at = rel[:, :keys]
                low = -(off + t * ROWS)
                sc = jnp.where((at >= low) & (at < low + reach), sc, FILL)
            return sc

        def soft(t, sc):
            m_old = m_sc[which, t]
            m_new = jnp.maximum(m_old, jnp.max(sc, axis=1, keepdims=True))
            alpha = jnp.exp2(m_old - m_new)
            p = jnp.exp2(sc - jnp.tile(m_new, (1, keys // HD)))
            m_sc[which, t] = m_new
            l_sc[which, t] = alpha * l_sc[which, t] + jnp.sum(p, axis=1, keepdims=True)
            return p.astype(BF), alpha

        def gather(t, p, alpha):
            acc_sc[which, t] = alpha * acc_sc[which, t] + jnp.dot(p, v, preferred_element_type=F32)

        current, pending = scores(0), None
        for t in range(4):
            following = scores(t + 1) if t < 3 else None
            weights = soft(t, current)
            if pending is not None:
                gather(*pending)
            pending = (t, *weights)
            current = following
        gather(*pending)

    def step(n, _):
        for unit in range(5, 16):

            @pl.when(n == unit - 4)
            def _(unit=unit):
                move_full(unit // 2, unit % 2)

        for at, moves in MOVES.items():

            @pl.when(n == at)
            def _(moves=moves):
                for kind, d in moves:
                    move_band(kind, d)

        for at, (which, d, other) in enumerate(TASKS):

            @pl.when(n == at)
            def _(which=which, d=d, other=other):
                if d == 0 and not other:
                    for j in range(4):
                        landed(qb.at[which, j], r_q.at[4 * which + j])
                if which == 0 and other:
                    when(z >= d, lambda: landed(kv.at[2 * d + 1 - c], r_sa.at[d]))
                if which == 1:
                    when(z >= d, lambda: landed(kv.at[6 + d, other2], r_sb.at[d]))
                if which == 2:
                    when(needed(d), lambda: landed(kv.at[9 + (z + d) % 8, other2], r_sf.at[d]))

        which = table(n, [t[0] for t in TASKS])
        d = table(n, [t[1] for t in TASKS])
        other = table(n, [t[2] for t in TASKS])
        side = jnp.where(other == 1, 1 - c, c)
        full = which == 2
        plane = jnp.where(full, (z + d) % 8, z - d)
        chunk = jnp.where(full, 9 + plane, jnp.where(which == 1, 6 + d, 2 * d + side))
        valid = jnp.where(full, (d == 0) | (plane < z), z >= d)
        parity = jnp.where(which == 0, side, par)
        off = q_start - plane * 8 * ROWS - parity * ROWS
        reach = jnp.where(full, 1 << 20, jnp.where(which == 1, reach_b, reach_a))
        lower = (d == 0) & (c == 0)
        upper = jnp.logical_not(full) & (d == 2) & (c == 1)
        plain = full & (d > 0)

        @pl.when(valid & plain)
        def _():
            absorb(which, chunk, 0, 4, off, reach, False)

        @pl.when(valid & jnp.logical_not(plain | lower | upper))
        def _():
            absorb(which, chunk, 0, 4, off, reach, True)

        @pl.when(valid & (lower | upper))
        def _():
            first = jnp.where(upper, 2, 0)
            absorb(which, chunk, first, 2, off - first * 2 * ROWS, reach, True)

        return 0

    lax.fori_loop(0, len(TASKS), step, 0)

    def send_back(t, _):
        for which in range(3):
            total = l_sc[which, t]
            safe = jnp.where(total > 0.0, total, 1.0)
            o[t, which] = (acc_sc[which, t] / safe).astype(BF)
            if which:
                level = jnp.where(total > 0.0, m_sc[which, t] + jnp.log2(safe), FILL)
                lse[t, which - 1] = level.T[:8]
        for back in backs(t):
            back.start()
        return 0

    def backs(t):
        home = base + 2 * (2 * c + t // 2) + t % 2
        return [
            Push(o.at[t], r.at[y], s_o.at[t], r_o.at[y], home, s, hd),
            Push(lse.at[t], rl.at[y], s_l.at[t], r_l.at[y], home, s, hd),
        ]

    lax.fori_loop(0, 4, send_back, 0)
    for i in range(4):
        landed(r.at[i], r_o.at[i])
        landed(rl.at[i], r_l.at[i])
    for i in range(4):
        merged[i] = r[i, 0]
    for which in range(2):
        for two in range(2):
            first, second = 2 * two, 2 * two + 1

            def column(i):
                return jnp.tile(rl[i, which], (16, 1)).T

            a, b = column(first), column(second)
            top = jnp.maximum(a, b)
            wa, wb = jnp.exp2(a - top), jnp.exp2(b - top)
            value = wa * r[first, which + 1].astype(F32) + wb * r[second, which + 1].astype(F32)
            merged[4 + 2 * which + two] = (value / (wa + wb)).astype(BF)
    for h in range(8):
        band = h - jnp.where(h > f0, 1, 0) - jnp.where(h > f1, 1, 0)
        slot = jnp.where(f0 == h, 6, jnp.where(f1 == h, 7, jnp.clip(band, 0, 5)))
        att[:, h * HD : (h + 1) * HD] = merged[slot]
    landed(wv, w_sem)

    def project(dest):
        for side in range(2):
            for sub in range(2):
                columns = pl.ds(pl.multiple_of(dest * 1024 + side * 512 + sub * 256, 256), 256)
                piece = jnp.dot(att[...], wv[:, columns], preferred_element_type=F32)
                part[dest, side, :, sub * 256 : (sub + 1) * 256] = piece.astype(BF)

    def ship(src, slot, target):
        one = pltpu.make_async_remote_copy(
            src_ref=src,
            dst_ref=got.at[slot],
            send_sem=s_x.at[slot],
            recv_sem=r_x.at[slot],
            device_id=(s, target),
            device_id_type=MESH,
        )
        one.start()
        return one

    across = (hd + 2) % 4
    project(across)
    moved = [ship(part.at[across, 0], 0, right), ship(part.at[across, 1], 1, left)]
    project(right)
    moved.append(ship(part.at[right, 1], 2, right))
    project(left)
    moved.append(ship(part.at[left, 0], 3, left))
    landed(got.at[0], r_x.at[0])
    tmp[0] = (got[0].astype(F32) + part[right, 0].astype(F32)).astype(BF)
    moved.append(ship(tmp.at[0], 4, right))
    landed(got.at[1], r_x.at[1])
    tmp[1] = (got[1].astype(F32) + part[left, 1].astype(F32)).astype(BF)
    moved.append(ship(tmp.at[1], 5, left))
    project(hd)
    for one in sends:
        one.wait_send()
    for h in range(7):
        for j in range(2):
            full_down(h, j).wait_send()
    for h in range(8):
        when(needed(h), full_sib(h).wait_send)
    for kind in ("a", "b"):
        for d in range(3):
            if d < 2:
                when((z >= d) & (z < 7), band_up(kind, d).wait_send)
            when(z >= d, band_sib(kind, d).wait_send)
    for t in range(4):
        for back in backs(t):
            back.wait_send()
    landed(got.at[2], r_x.at[2])
    landed(got.at[3], r_x.at[3])
    landed(got.at[4], r_x.at[4])
    out[:, :512] = (part[hd, 0].astype(F32) + got[4].astype(F32) + got[3].astype(F32)).astype(BF)
    landed(got.at[5], r_x.at[5])
    out[:, 512:] = (part[hd, 1].astype(F32) + got[5].astype(F32) + got[2].astype(F32)).astype(BF)
    for one in moved:
        one.wait_send()


def whole(full_ids, spans, qh, kvh, w):
    dma = pltpu.SemaphoreType.DMA
    counts = (8, 8, 12, 12, 2, 2, 2, 2, 14, 14, 3, 3, 3, 3, 8, 8, 4, 4, 4, 4, 6, 6)
    smem = pl.BlockSpec(memory_space=pltpu.SMEM)
    return pl.pallas_call(
        whole_body,
        out_shape=jax.ShapeDtypeStruct((ROWS, 1024), BF),
        in_specs=[smem, smem, ANY, ANY, ANY],
        out_specs=VM,
        scratch_shapes=[
            pltpu.VMEM((1024, 4096), BF),
            pltpu.VMEM((17, 4, 2, ROWS, HD), BF),
            pltpu.VMEM((3, 4, ROWS, HD), BF),
            pltpu.VMEM((4, 3, ROWS, HD), BF),
            pltpu.VMEM((4, 2, 8, ROWS), F32),
            pltpu.VMEM((4, 3, ROWS, HD), BF),
            pltpu.VMEM((4, 2, 8, ROWS), F32),
            pltpu.VMEM((8, ROWS, HD), BF),
            pltpu.VMEM((ROWS, 1024), BF),
            pltpu.VMEM((4, 2, ROWS, 512), BF),
            pltpu.VMEM((6, ROWS, 512), BF),
            pltpu.VMEM((2, ROWS, 512), BF),
            pltpu.VMEM((3, 4, ROWS, HD), F32),
            pltpu.VMEM((3, 4, ROWS, HD), F32),
            pltpu.VMEM((3, 4, ROWS, HD), F32),
            pltpu.VMEM((ROWS, 4 * ROWS), jnp.int32),
            dma(()),
        ]
        + [dma((n,)) for n in counts],
        compiler_params=pltpu.CompilerParams(collective_id=0, has_side_effects=True, vmem_limit_bytes=56 << 20),
        name="whole",
    )(full_ids, spans, qh, kvh, w)


def on_device(queries, keys_in, values_in, out_weight, spans, full_ids):
    qh, kvh = arrange(full_ids, queries, keys_in, values_in)
    return whole(full_ids, spans, qh, kvh, out_weight)


def solution(mesh):
    placed = (P("seq", "head"), P("seq", "head"), P("seq", "head"), P("head", None), P("head"), P("head"))
    return jax.shard_map(on_device, mesh=mesh, in_specs=placed, out_specs=P("seq", "head"), check_vma=False)
```

```python
import functools
import math

import jax
import jax.numpy as jnp
from jax import lax
from jax.experimental import pallas as pl
from jax.experimental.pallas import tpu as pltpu
from jax.sharding import PartitionSpec as P

HD = 128
ROWS = 256
SCALE2 = HD ** (-0.5) * math.log2(math.e)
FILL = -1e30
FLOOR = -5e29
MESH = pl.DeviceIdType.MESH
ANY = pl.BlockSpec(memory_space=pl.ANY)
VM = pl.BlockSpec(memory_space=pltpu.VMEM)
BF = jnp.bfloat16
F32 = jnp.float32


def position():
    s = lax.axis_index("seq")
    return s, s // 8, (s // 2) % 4, s % 2, lax.axis_index("head")


def pick(slot, f0, f1):
    h = slot + (slot >= f0).astype(jnp.int32)
    h = h + (h >= f1).astype(jnp.int32)
    return jnp.where(slot == 6, f0, jnp.where(slot == 7, f1, h))


def greet(targets):
    barrier = pltpu.get_barrier_semaphore()
    for target in targets:
        pl.semaphore_signal(barrier, inc=1, device_id=target, device_id_type=MESH)
    pl.semaphore_wait(barrier, len(targets))


def plane_peers(s, hd):
    base = (s // 8) * 8
    return [(base + (s + r) % 8, hd) for r in range(1, 8)]


class Push:
    def __init__(self, src, dst, ssem, rsem, target, me, hd):
        self.remote = pltpu.make_async_remote_copy(
            src_ref=src, dst_ref=dst, send_sem=ssem, recv_sem=rsem, device_id=(target, hd), device_id_type=MESH
        )
        self.local = pltpu.make_async_copy(src, dst, rsem)
        self.away = target != me

    def start(self):
        @pl.when(self.away)
        def _():
            self.remote.start()

        @pl.when(jnp.logical_not(self.away))
        def _():
            self.local.start()

    def wait_send(self):
        @pl.when(self.away)
        def _():
            self.remote.wait_send()


def landed(ref, sem):
    pltpu.make_async_copy(ref, ref, sem).wait()


TASKS = (
    (0, 0, 0),
    (0, 0, 1),
    (2, 0, 0),
    (2, 1, 0),
    (1, 0, 0),
    (2, 2, 0),
    (0, 1, 0),
    (2, 3, 0),
    (0, 1, 1),
    (2, 4, 0),
    (1, 1, 0),
    (2, 5, 0),
    (0, 2, 0),
    (0, 2, 1),
    (2, 6, 0),
    (1, 2, 0),
    (2, 7, 0),
)
MOVES = {3: (("b", 0),), 4: (("a", 1),), 8: (("b", 1),), 12: (("a", 2),), 14: (("b", 2),)}
DONE = {14: 0, 16: 1}


def table(n, values):
    out = jnp.int32(values[0])
    for i, value in enumerate(values[1:], 1):
        out = jnp.where(n == i, value, out)
    return out


def whole_body(
    ids, spans, queries, keys_in, values_in, w, out,
    qh, kvh, wv, kv, qb, o, lse, r, rl, merged, att, part, got, tmp, m_sc, l_sc, acc_sc, rel,
    w_sem, s_in, r_in, s_q, r_q, s_fa, r_fa, s_fb, r_fb, s_ff, r_ff, s_sa, r_sa, s_sb, r_sb, s_sf, r_sf,
    s_o, r_o, s_l, r_l, s_x, r_x,
):
    s, z, y, c, hd = position()
    pair, par = y // 2, y % 2
    base = z * 8
    up, down = (s + 8) % 64, (s + 56) % 64
    sib = base + 2 * y + (1 - c)
    right, left = (hd + 1) % 4, (hd + 3) % 4
    half = y // 2
    pltpu.make_async_copy(w, wv, w_sem).start()
    f0, f1 = ids[0] - hd * 8, ids[1] - hd * 8

    def column_of(ref, slot):
        h = pick(jnp.int32(slot), f0, f1)
        first, last = (slot, slot + 2) if slot < 6 else (slot - 6, slot)
        out = ref[:, last * HD : (last + 1) * HD]
        for i in range(first, last):
            out = jnp.where(h == i, ref[:, i * HD : (i + 1) * HD], out)
        return out

    def arrange_kv(slots):
        for i in slots:
            kvh[i, 0] = column_of(keys_in, i)
            kvh[i, 1] = column_of(values_in, i)

    def arrange_q(slots):
        for i in slots:
            qh[i] = column_of(queries, i)

    arrange_kv((6, 7))
    opposite = [((7 - z) * 8 + i, hd) for i in range(8)]
    greet(plane_peers(s, hd) + [(up, hd), (down, hd), (s, right), (s, left)] + opposite)

    sends = []

    def push(src, dst, ssem, rsem, target):
        one = Push(src, dst, ssem, rsem, target, s, hd)
        one.start()
        sends.append(one)

    def push_q(i, slot):
        for t in range(4):
            there = jnp.where(c == 1, 7 - z, z) * 8 if i == 2 else base
            push(qh.at[slot(t)], qb.at[i, place], s_q.at[4 * i + t], r_q.at[4 * i + place], there + 2 * t + half)

    place = 2 * (y % 2) + c
    def prepare():
        row = lax.broadcasted_iota(jnp.int32, (ROWS, 4 * ROWS), 0)
        col = lax.broadcasted_iota(jnp.int32, (ROWS, 4 * ROWS), 1)
        rel[...] = row - col - (col // ROWS) * ROWS
        m_sc[...] = jnp.full_like(m_sc, FLOOR)
        l_sc[...] = jnp.zeros_like(l_sc)
        acc_sc[...] = jnp.zeros_like(acc_sc)

    def hop(src, dst, ssem, rsem, target):
        return pltpu.make_async_remote_copy(
            src_ref=src, dst_ref=dst, send_sem=ssem, recv_sem=rsem, device_id=(target, hd), device_id_type=MESH
        )

    def when(cond, action):
        pl.when(cond)(action)

    mine2 = pl.ds(2 * c, 2)
    other2 = pl.ds(2 * (1 - c), 2)

    def full_down(h, j):
        ref = kv.at[9 + (z + h) % 8, 2 * c + j]
        return hop(ref, ref, s_ff.at[2 * h + j], r_ff.at[2 * h + j], down)

    def full_sib(h):
        ref = kv.at[9 + (z + h) % 8, mine2]
        return hop(ref, ref, s_sf.at[h], r_sf.at[h], sib)

    def needed(h):
        return (z + h) % 8 <= jnp.maximum(z, 7 - z)

    def move_full(h, j):
        ref = kv.at[9 + (z + h) % 8, 2 * c + j]
        landed(ref, r_in.at[j] if h == 0 else r_ff.at[2 * h - 2 + j])
        if h < 7:
            full_down(h, j).start()
        if j == 1:
            when(needed(h), full_sib(h).start)

    def band_up(kind, d):
        if kind == "a":
            return hop(kv.at[2 * d + c], kv.at[2 * d + 2 + c], s_fa.at[d], r_fa.at[d], up)
        return hop(kv.at[6 + d, mine2], kv.at[7 + d, mine2], s_fb.at[d], r_fb.at[d], up)

    def band_sib(kind, d):
        if kind == "a":
            return hop(kv.at[2 * d + c], kv.at[2 * d + c], s_sa.at[d], r_sa.at[d], sib)
        return hop(kv.at[6 + d, mine2], kv.at[6 + d, mine2], s_sb.at[d], r_sb.at[d], sib)

    def move_band(kind, d):
        if d == 0 and kind == "a":
            for j in range(4):
                landed(kv.at[c, j], r_in.at[2 + j])
        elif d == 0:
            for j in range(2):
                landed(kv.at[6, 2 * c + j], r_in.at[6 + j])
        else:

            @pl.when(z >= d)
            def _():
                if kind == "a":
                    landed(kv.at[2 * d + c], r_fa.at[d - 1])
                else:
                    landed(kv.at[6 + d, mine2], r_fb.at[d - 1])

        if d < 2:
            when((z >= d) & (z < 7), band_up(kind, d).start)
        when(z >= d, band_sib(kind, d).start)

    for g in range(2):
        push(kvh.at[6 + g], kv.at[9 + z, y], s_in.at[g], r_in.at[y % 2], base + 2 * (2 * g + c) + half)
    arrange_kv(range(4))
    arrange_q(range(4))
    move_full(0, 0)
    move_full(0, 1)
    for t in range(4):
        push(kvh.at[t], kv.at[c, y], s_in.at[2 + t], r_in.at[2 + y], base + 2 * t + c)
    push_q(0, lambda t: t)
    arrange_kv((4, 5))
    arrange_q(range(4, 8))
    prepare()
    move_full(1, 0)
    move_band("a", 0)
    push_q(2, lambda t: 6 + t // 2)
    for g in range(2):
        push(kvh.at[4 + g], kv.at[6, y], s_in.at[6 + g], r_in.at[6 + y % 2], base + 2 * (2 * g + c) + half)
    move_full(1, 1)
    move_full(2, 0)
    push_q(1, lambda t: 4 + t // 2)

    reach_a = spans[jnp.clip(pick(y, f0, f1), 0, 7)]
    reach_b = spans[jnp.clip(pick(4 + pair, f0, f1), 0, 7)]
    q_start = base * ROWS + c * 4 * ROWS

    def absorb(which, chunk, first, units, tiles, off, skew, reach, masked):
        keys = units * ROWS
        k = kv[chunk, pl.ds(first, units), 0].reshape(keys, HD)
        v = kv[chunk, pl.ds(first, units), 1].reshape(keys, HD)

        def scores(t):
            sc = SCALE2 * lax.dot_general(
                qb[which, t], k, (((1,), (1,)), ((), ())), preferred_element_type=F32
            )
            if masked:
                at = rel[:, :keys]
                low = -(off + t * ROWS + (t % 2) * skew)
                sc = jnp.where((at >= low) & (at < low + reach), sc, FILL)
            return sc

        def soft(t, sc):
            m_old = m_sc[which, t]
            m_new = jnp.maximum(m_old, jnp.max(sc, axis=1, keepdims=True))
            alpha = jnp.exp2(m_old - m_new)
            p = jnp.exp2(sc - jnp.tile(m_new, (1, keys // HD)))
            m_sc[which, t] = m_new
            l_sc[which, t] = alpha * l_sc[which, t] + jnp.sum(p, axis=1, keepdims=True)
            return p.astype(BF), alpha

        def gather(t, p, alpha):
            acc_sc[which, t] = alpha * acc_sc[which, t] + jnp.dot(p, v, preferred_element_type=F32)

        current, pending = scores(tiles[0]), None
        for i, t in enumerate(tiles):
            following = scores(tiles[i + 1]) if i + 1 < len(tiles) else None
            weights = soft(t, current)
            if pending is not None:
                gather(*pending)
            pending = (t, *weights)
            current = following
        gather(*pending)

    def step(n, _):
        for unit in range(5, 16):

            @pl.when(n == unit - 4)
            def _(unit=unit):
                move_full(unit // 2, unit % 2)

        for at, moves in MOVES.items():

            @pl.when(n == at)
            def _(moves=moves):
                for kind, d in moves:
                    move_band(kind, d)

        for at, which in DONE.items():

            @pl.when(n == at)
            def _(which=which):
                send_back(which)

        for at, (which, d, other) in enumerate(TASKS):

            @pl.when(n == at)
            def _(which=which, d=d, other=other):
                if d == 0 and not other:
                    for j in range(4):
                        landed(qb.at[which, j], r_q.at[4 * which + j])
                if which == 0 and other:
                    when(z >= d, lambda: landed(kv.at[2 * d + 1 - c], r_sa.at[d]))
                if which == 1:
                    when(z >= d, lambda: landed(kv.at[6 + d, other2], r_sb.at[d]))
                if which == 2:
                    when(needed(d), lambda: landed(kv.at[9 + (z + d) % 8, other2], r_sf.at[d]))

        which = table(n, [t[0] for t in TASKS])
        d = table(n, [t[1] for t in TASKS])
        other = table(n, [t[2] for t in TASKS])
        side = jnp.where(other == 1, 1 - c, c)
        full = which == 2
        plane = jnp.where(full, (z + d) % 8, z - d)
        chunk = jnp.where(full, 9 + plane, jnp.where(which == 1, 6 + d, 2 * d + side))
        own, mirror = plane <= z, plane <= 7 - z
        quad = jnp.where(full, own & mirror, z >= d)
        pair_only = full & (own != mirror)
        parity = jnp.where(which == 0, side, par)
        off = q_start - plane * 8 * ROWS - parity * ROWS
        reach = jnp.where(full, 1 << 20, jnp.where(which == 1, reach_b, reach_a))
        skew = jnp.where(full, (7 - 2 * z) * 8 * ROWS, 0)
        lower = jnp.logical_not(full) & (d == 0) & (c == 0)
        upper = jnp.logical_not(full) & (d == 2) & (c == 1)
        plain = full & (plane != z) & (plane != 7 - z)
        four = (0, 1, 2, 3)

        @pl.when(quad & plain)
        def _():
            absorb(which, chunk, 0, 4, four, off, skew, reach, False)

        @pl.when(quad & jnp.logical_not(plain | lower | upper))
        def _():
            absorb(which, chunk, 0, 4, four, off, skew, reach, True)

        @pl.when(quad & (lower | upper))
        def _():
            first = jnp.where(upper, 2, 0)
            absorb(which, chunk, first, 2, four, off - first * 2 * ROWS, skew, reach, True)

        start = jnp.where(own, 0, 1)

        @pl.when(pair_only & plain)
        def _():
            absorb(which, chunk, 0, 4, (start, start + 2), off, skew, reach, False)

        @pl.when(pair_only & jnp.logical_not(plain))
        def _():
            absorb(which, chunk, 0, 4, (start, start + 2), off, skew, reach, True)

        return 0

    def backs(which, t):
        there = jnp.where(t % 2 == 1, 7 - z, z) * 8 if which == 2 else base
        home = there + 2 * (2 * c + t // 2) + t % 2
        i = 4 * which
        out = [Push(o.at[which, t], r.at[which, y], s_o.at[i + t], r_o.at[i + y], home, s, hd)]
        if which:
            i -= 4
            out.append(Push(lse.at[which - 1, t], rl.at[which - 1, y], s_l.at[i + t], r_l.at[i + y], home, s, hd))
        return out

    def send_back(which):
        def one(t, _):
            total = l_sc[which, t]
            safe = jnp.where(total > 0.0, total, 1.0)
            o[which, t] = (acc_sc[which, t] / safe).astype(BF)
            if which:
                level = jnp.where(total > 0.0, m_sc[which, t] + jnp.log2(safe), FILL)
                lse[which - 1, t] = level.T[:8]
            for back in backs(which, t):
                back.start()
            return 0

        lax.fori_loop(0, 4, one, 0)

    lax.fori_loop(0, len(TASKS), step, 0)
    send_back(2)
    for i in range(4):
        landed(r.at[0, i], r_o.at[i])
        merged[i] = r[0, i]
    for which in range(2):
        for i in range(4):
            landed(r.at[which + 1, i], r_o.at[4 * which + 4 + i])
            landed(rl.at[which, i], r_l.at[4 * which + i])
        for two in range(2):
            first, second = 2 * two, 2 * two + 1

            def column(i):
                return jnp.tile(rl[which, i], (16, 1)).T

            a, b = column(first), column(second)
            top = jnp.maximum(a, b)
            wa, wb = jnp.exp2(a - top), jnp.exp2(b - top)
            value = wa * r[which + 1, first].astype(F32) + wb * r[which + 1, second].astype(F32)
            merged[4 + 2 * which + two] = (value / (wa + wb)).astype(BF)
    for h in range(8):
        band = h - jnp.where(h > f0, 1, 0) - jnp.where(h > f1, 1, 0)
        slot = jnp.where(f0 == h, 6, jnp.where(f1 == h, 7, jnp.clip(band, 0, 5)))
        att[:, h * HD : (h + 1) * HD] = merged[slot]
    landed(wv, w_sem)

    def project(dest):
        for side in range(2):
            for sub in range(2):
                columns = pl.ds(pl.multiple_of(dest * 1024 + side * 512 + sub * 256, 256), 256)
                piece = jnp.dot(att[...], wv[:, columns], preferred_element_type=F32)
                part[dest, side, :, sub * 256 : (sub + 1) * 256] = piece.astype(BF)

    def ship(src, slot, target):
        one = pltpu.make_async_remote_copy(
            src_ref=src,
            dst_ref=got.at[slot],
            send_sem=s_x.at[slot],
            recv_sem=r_x.at[slot],
            device_id=(s, target),
            device_id_type=MESH,
        )
        one.start()
        return one

    across = (hd + 2) % 4
    project(across)
    moved = [ship(part.at[across, 0], 0, right), ship(part.at[across, 1], 1, left)]
    project(right)
    moved.append(ship(part.at[right, 1], 2, right))
    project(left)
    moved.append(ship(part.at[left, 0], 3, left))
    landed(got.at[0], r_x.at[0])
    tmp[0] = (got[0].astype(F32) + part[right, 0].astype(F32)).astype(BF)
    moved.append(ship(tmp.at[0], 4, right))
    landed(got.at[1], r_x.at[1])
    tmp[1] = (got[1].astype(F32) + part[left, 1].astype(F32)).astype(BF)
    moved.append(ship(tmp.at[1], 5, left))
    project(hd)
    for one in sends:
        one.wait_send()
    for h in range(7):
        for j in range(2):
            full_down(h, j).wait_send()
    for h in range(8):
        when(needed(h), full_sib(h).wait_send)
    for kind in ("a", "b"):
        for d in range(3):
            if d < 2:
                when((z >= d) & (z < 7), band_up(kind, d).wait_send)
            when(z >= d, band_sib(kind, d).wait_send)
    for which in range(3):
        for t in range(4):
            for back in backs(which, t):
                back.wait_send()
    landed(got.at[2], r_x.at[2])
    landed(got.at[3], r_x.at[3])
    landed(got.at[4], r_x.at[4])
    out[:, :512] = (part[hd, 0].astype(F32) + got[4].astype(F32) + got[3].astype(F32)).astype(BF)
    landed(got.at[5], r_x.at[5])
    out[:, 512:] = (part[hd, 1].astype(F32) + got[5].astype(F32) + got[2].astype(F32)).astype(BF)
    for one in moved:
        one.wait_send()


def whole(full_ids, spans, queries, keys_in, values_in, w):
    dma = pltpu.SemaphoreType.DMA
    counts = (8, 8, 12, 12, 2, 2, 2, 2, 14, 14, 3, 3, 3, 3, 8, 8, 12, 12, 8, 8, 6, 6)
    smem = pl.BlockSpec(memory_space=pltpu.SMEM)
    return pl.pallas_call(
        whole_body,
        out_shape=jax.ShapeDtypeStruct((ROWS, 1024), BF),
        in_specs=[smem, smem, VM, VM, VM, ANY],
        out_specs=VM,
        scratch_shapes=[
            pltpu.VMEM((8, ROWS, HD), BF),
            pltpu.VMEM((8, 2, ROWS, HD), BF),
            pltpu.VMEM((1024, 4096), BF),
            pltpu.VMEM((17, 4, 2, ROWS, HD), BF),
            pltpu.VMEM((3, 4, ROWS, HD), BF),
            pltpu.VMEM((3, 4, ROWS, HD), BF),
            pltpu.VMEM((2, 4, 8, ROWS), F32),
            pltpu.VMEM((3, 4, ROWS, HD), BF),
            pltpu.VMEM((2, 4, 8, ROWS), F32),
            pltpu.VMEM((8, ROWS, HD), BF),
            pltpu.VMEM((ROWS, 1024), BF),
            pltpu.VMEM((4, 2, ROWS, 512), BF),
            pltpu.VMEM((6, ROWS, 512), BF),
            pltpu.VMEM((2, ROWS, 512), BF),
            pltpu.VMEM((3, 4, ROWS, HD), F32),
            pltpu.VMEM((3, 4, ROWS, HD), F32),
            pltpu.VMEM((3, 4, ROWS, HD), F32),
            pltpu.VMEM((ROWS, 4 * ROWS), jnp.int32),
            dma(()),
        ]
        + [dma((n,)) for n in counts],
        compiler_params=pltpu.CompilerParams(collective_id=0, has_side_effects=True, vmem_limit_bytes=56 << 20),
        name="whole",
    )(full_ids, spans, queries, keys_in, values_in, w)


def on_device(queries, keys_in, values_in, out_weight, spans, full_ids):
    return whole(full_ids, spans, queries, keys_in, values_in, out_weight)


def solution(mesh):
    placed = (P("seq", "head"), P("seq", "head"), P("seq", "head"), P("head", None), P("head"), P("head"))
    return jax.shard_map(on_device, mesh=mesh, in_specs=placed, out_specs=P("seq", "head"), check_vma=False)
```

```python
import functools
import math

import jax
import jax.numpy as jnp
from jax import lax
from jax.experimental import pallas as pl
from jax.experimental.pallas import tpu as pltpu
from jax.sharding import PartitionSpec as P

HD = 128
ROWS = 256
SCALE2 = HD ** (-0.5) * math.log2(math.e)
FILL = -1e30
FLOOR = -5e29
MESH = pl.DeviceIdType.MESH
ANY = pl.BlockSpec(memory_space=pl.ANY)
VM = pl.BlockSpec(memory_space=pltpu.VMEM)
BF = jnp.bfloat16
F32 = jnp.float32


def position():
    s = lax.axis_index("seq")
    return s, s // 8, (s // 2) % 4, s % 2, lax.axis_index("head")


def pick(slot, f0, f1):
    h = slot + (slot >= f0).astype(jnp.int32)
    h = h + (h >= f1).astype(jnp.int32)
    return jnp.where(slot == 6, f0, jnp.where(slot == 7, f1, h))


def greet(targets):
    barrier = pltpu.get_barrier_semaphore()
    for target in targets:
        pl.semaphore_signal(barrier, inc=1, device_id=target, device_id_type=MESH)
    pl.semaphore_wait(barrier, len(targets))


def plane_peers(s, hd):
    base = (s // 8) * 8
    return [(base + (s + r) % 8, hd) for r in range(1, 8)]


class Push:
    def __init__(self, src, dst, ssem, rsem, target, me, hd):
        self.remote = pltpu.make_async_remote_copy(
            src_ref=src, dst_ref=dst, send_sem=ssem, recv_sem=rsem, device_id=(target, hd), device_id_type=MESH
        )
        self.local = pltpu.make_async_copy(src, dst, rsem)
        self.away = target != me

    def start(self):
        @pl.when(self.away)
        def _():
            self.remote.start()

        @pl.when(jnp.logical_not(self.away))
        def _():
            self.local.start()

    def wait_send(self):
        @pl.when(self.away)
        def _():
            self.remote.wait_send()


def landed(ref, sem):
    pltpu.make_async_copy(ref, ref, sem).wait()


TASKS = (
    (0, 0, 0),
    (0, 0, 1),
    (2, 0, 0),
    (2, 7, 0),
    (1, 0, 0),
    (2, 1, 0),
    (0, 1, 0),
    (2, 2, 0),
    (0, 1, 1),
    (2, 3, 0),
    (1, 1, 0),
    (2, 4, 0),
    (2, 5, 0),
    (0, 2, 0),
    (2, 6, 0),
    (0, 2, 1),
    (1, 2, 0),
)
MOVES = {2: (("f", 7),), 3: (("b", 0),), 4: (("a", 1),), 8: (("b", 1),), 12: (("a", 2),), 15: (("b", 2),)}
DONE = {15: 2, 16: 0}


def table(n, values):
    out = jnp.int32(values[0])
    for i, value in enumerate(values[1:], 1):
        out = jnp.where(n == i, value, out)
    return out


def whole_body(
    ids, spans, queries, keys_in, values_in, w, out,
    qh, kvh, wv, kv, qb, o, lse, r, rl, merged, att, part, got, tmp, m_sc, l_sc, acc_sc, rel,
    w_sem, s_in, r_in, s_q, r_q, s_fa, r_fa, s_fb, r_fb, s_ff, r_ff, s_fu, r_fu, s_sa, r_sa, s_sb, r_sb, s_sf, r_sf,
    s_o, r_o, s_l, r_l, s_x, r_x,
):
    s, z, y, c, hd = position()
    pair, par = y // 2, y % 2
    base = z * 8
    up, down = (s + 8) % 64, (s + 56) % 64
    sib = base + 2 * y + (1 - c)
    right, left = (hd + 1) % 4, (hd + 3) % 4
    half = y // 2
    pltpu.make_async_copy(w, wv, w_sem).start()
    f0, f1 = ids[0] - hd * 8, ids[1] - hd * 8

    def column_of(ref, slot):
        h = pick(jnp.int32(slot), f0, f1)
        first, last = (slot, slot + 2) if slot < 6 else (slot - 6, slot)
        out = ref[:, last * HD : (last + 1) * HD]
        for i in range(first, last):
            out = jnp.where(h == i, ref[:, i * HD : (i + 1) * HD], out)
        return out

    def arrange_kv(slots):
        for i in slots:
            kvh[i, 0] = column_of(keys_in, i)
            kvh[i, 1] = column_of(values_in, i)

    def arrange_q(slots):
        for i in slots:
            qh[i] = column_of(queries, i)

    arrange_kv((6, 7))
    greet(plane_peers(s, hd) + [(up, hd), (down, hd), (s, right), (s, left)])

    sends = []

    def push(src, dst, ssem, rsem, target):
        one = Push(src, dst, ssem, rsem, target, s, hd)
        one.start()
        sends.append(one)

    def push_q(i, slot):
        for t in range(4):
            push(qh.at[slot(t)], qb.at[i, place], s_q.at[4 * i + t], r_q.at[4 * i + place], base + 2 * t + half)

    place = 2 * (y % 2) + c
    def prepare():
        row = lax.broadcasted_iota(jnp.int32, (ROWS, 4 * ROWS), 0)
        col = lax.broadcasted_iota(jnp.int32, (ROWS, 4 * ROWS), 1)
        rel[...] = row - col - (col // ROWS) * ROWS
        m_sc[...] = jnp.full_like(m_sc, FLOOR)
        l_sc[...] = jnp.zeros_like(l_sc)
        acc_sc[...] = jnp.zeros_like(acc_sc)

    def hop(src, dst, ssem, rsem, target):
        return pltpu.make_async_remote_copy(
            src_ref=src, dst_ref=dst, send_sem=ssem, recv_sem=rsem, device_id=(target, hd), device_id_type=MESH
        )

    def when(cond, action):
        pl.when(cond)(action)

    mine2 = pl.ds(2 * c, 2)
    other2 = pl.ds(2 * (1 - c), 2)

    def full_down(h, j):
        ref = kv.at[9 + (z + h) % 8, 2 * c + j]
        return hop(ref, ref, s_ff.at[2 * h + j], r_ff.at[2 * h + j], down)

    def full_sib(h):
        ref = kv.at[9 + (z + h) % 8, mine2]
        return hop(ref, ref, s_sf.at[h], r_sf.at[h], sib)

    def needed(h):
        return (z + h) % 8 <= z

    def full_up(j):
        ref = kv.at[9 + z, 2 * c + j]
        return hop(ref, ref, s_fu.at[j], r_fu.at[j], up)

    def move_full(h, j):
        ref = kv.at[9 + (z + h) % 8, 2 * c + j]
        landed(ref, r_in.at[j] if h == 0 else r_fu.at[j] if h == 7 else r_ff.at[2 * h - 2 + j])
        if h < 6:
            full_down(h, j).start()
        if h == 0:
            full_up(j).start()
        if j == 1:
            when(needed(h), full_sib(h).start)

    def band_up(kind, d):
        if kind == "a":
            return hop(kv.at[2 * d + c], kv.at[2 * d + 2 + c], s_fa.at[d], r_fa.at[d], up)
        return hop(kv.at[6 + d, mine2], kv.at[7 + d, mine2], s_fb.at[d], r_fb.at[d], up)

    def band_sib(kind, d):
        if kind == "a":
            return hop(kv.at[2 * d + c], kv.at[2 * d + c], s_sa.at[d], r_sa.at[d], sib)
        return hop(kv.at[6 + d, mine2], kv.at[6 + d, mine2], s_sb.at[d], r_sb.at[d], sib)

    def move_band(kind, d):
        if d == 0 and kind == "a":
            for j in range(4):
                landed(kv.at[c, j], r_in.at[2 + j])
        elif d == 0:
            for j in range(2):
                landed(kv.at[6, 2 * c + j], r_in.at[6 + j])
        else:

            @pl.when(z >= d)
            def _():
                if kind == "a":
                    landed(kv.at[2 * d + c], r_fa.at[d - 1])
                else:
                    landed(kv.at[6 + d, mine2], r_fb.at[d - 1])

        if d < 2:
            when((z >= d) & (z < 7), band_up(kind, d).start)
        when(z >= d, band_sib(kind, d).start)

    for g in range(2):
        push(kvh.at[6 + g], kv.at[9 + z, y], s_in.at[g], r_in.at[y % 2], base + 2 * (2 * g + c) + half)
    arrange_kv(range(4))
    arrange_q(range(4))
    move_full(0, 0)
    move_full(0, 1)
    for t in range(4):
        push(kvh.at[t], kv.at[c, y], s_in.at[2 + t], r_in.at[2 + y], base + 2 * t + c)
    push_q(0, lambda t: t)
    arrange_kv((4, 5))
    arrange_q(range(4, 8))
    prepare()
    move_full(1, 0)
    move_band("a", 0)
    push_q(2, lambda t: 6 + t // 2)
    for g in range(2):
        push(kvh.at[4 + g], kv.at[6, y], s_in.at[6 + g], r_in.at[6 + y % 2], base + 2 * (2 * g + c) + half)
    move_full(1, 1)
    move_full(2, 0)
    push_q(1, lambda t: 4 + t // 2)

    reach_a = spans[jnp.clip(pick(y, f0, f1), 0, 7)]
    reach_b = spans[jnp.clip(pick(4 + pair, f0, f1), 0, 7)]
    q_start = base * ROWS + c * 4 * ROWS

    def absorb(which, chunk, first, units, off, reach, masked):
        keys = units * ROWS
        k = kv[chunk, pl.ds(first, units), 0].reshape(keys, HD)
        v = kv[chunk, pl.ds(first, units), 1].reshape(keys, HD)

        def scores(t):
            sc = SCALE2 * lax.dot_general(
                qb[which, t], k, (((1,), (1,)), ((), ())), preferred_element_type=F32
            )
            if masked:
                at = rel[:, :keys]
                low = -(off + t * ROWS)
                sc = jnp.where((at >= low) & (at < low + reach), sc, FILL)
            return sc

        def soft(t, sc):
            m_old = m_sc[which, t]
            m_new = jnp.maximum(m_old, jnp.max(sc, axis=1, keepdims=True))
            alpha = jnp.exp2(m_old - m_new)
            p = jnp.exp2(sc - jnp.tile(m_new, (1, keys // HD)))
            m_sc[which, t] = m_new
            l_sc[which, t] = alpha * l_sc[which, t] + jnp.sum(p, axis=1, keepdims=True)
            return p.astype(BF), alpha

        def gather(t, p, alpha):
            acc_sc[which, t] = alpha * acc_sc[which, t] + jnp.dot(p, v, preferred_element_type=F32)

        current, pending = scores(0), None
        for t in range(4):
            following = scores(t + 1) if t < 3 else None
            weights = soft(t, current)
            if pending is not None:
                gather(*pending)
            pending = (t, *weights)
            current = following
        gather(*pending)

    def step(n, _):
        for unit in range(5, 14):

            @pl.when(n == unit - 4)
            def _(unit=unit):
                move_full(unit // 2, unit % 2)

        for at, moves in MOVES.items():

            @pl.when(n == at)
            def _(moves=moves):
                for kind, d in moves:
                    if kind == "f":
                        move_full(d, 0)
                        move_full(d, 1)
                    else:
                        move_band(kind, d)

        for at, which in DONE.items():

            @pl.when(n == at)
            def _(which=which):
                send_back(which)

        for at, (which, d, other) in enumerate(TASKS):

            @pl.when(n == at)
            def _(which=which, d=d, other=other):
                if d == 0 and not other:
                    for j in range(4):
                        landed(qb.at[which, j], r_q.at[4 * which + j])
                if which == 0 and other:
                    when(z >= d, lambda: landed(kv.at[2 * d + 1 - c], r_sa.at[d]))
                if which == 1:
                    when(z >= d, lambda: landed(kv.at[6 + d, other2], r_sb.at[d]))
                if which == 2:
                    when(needed(d), lambda: landed(kv.at[9 + (z + d) % 8, other2], r_sf.at[d]))

        which = table(n, [t[0] for t in TASKS])
        d = table(n, [t[1] for t in TASKS])
        other = table(n, [t[2] for t in TASKS])
        side = jnp.where(other == 1, 1 - c, c)
        full = which == 2
        plane = jnp.where(full, (z + d) % 8, z - d)
        chunk = jnp.where(full, 9 + plane, jnp.where(which == 1, 6 + d, 2 * d + side))
        valid = jnp.where(full, plane <= z, z >= d)
        parity = jnp.where(which == 0, side, par)
        off = q_start - plane * 8 * ROWS - parity * ROWS
        reach = jnp.where(full, 1 << 20, jnp.where(which == 1, reach_b, reach_a))
        lower = (d == 0) & (c == 0)
        upper = jnp.logical_not(full) & (d == 2) & (c == 1)
        plain = full & (d > 0)

        @pl.when(valid & plain)
        def _():
            absorb(which, chunk, 0, 4, off, reach, False)

        @pl.when(valid & jnp.logical_not(plain | lower | upper))
        def _():
            absorb(which, chunk, 0, 4, off, reach, True)

        @pl.when(valid & (lower | upper))
        def _():
            first = jnp.where(upper, 2, 0)
            absorb(which, chunk, first, 2, off - first * 2 * ROWS, reach, True)

        return 0

    def backs(which, t):
        home = base + 2 * (2 * c + t // 2) + t % 2
        i = 4 * which
        out = [Push(o.at[which, t], r.at[which, y], s_o.at[i + t], r_o.at[i + y], home, s, hd)]
        if which:
            i -= 4
            out.append(Push(lse.at[which - 1, t], rl.at[which - 1, y], s_l.at[i + t], r_l.at[i + y], home, s, hd))
        return out

    def send_back(which):
        def one(t, _):
            total = l_sc[which, t]
            safe = jnp.where(total > 0.0, total, 1.0)
            o[which, t] = (acc_sc[which, t] / safe).astype(BF)
            if which:
                level = jnp.where(total > 0.0, m_sc[which, t] + jnp.log2(safe), FILL)
                lse[which - 1, t] = level.T[:8]
            for back in backs(which, t):
                back.start()
            return 0

        lax.fori_loop(0, 4, one, 0)

    lax.fori_loop(0, len(TASKS), step, 0)
    send_back(1)
    for i in range(4):
        landed(r.at[0, i], r_o.at[i])
        merged[i] = r[0, i]
    for which in range(2):
        for i in range(4):
            landed(r.at[which + 1, i], r_o.at[4 * which + 4 + i])
            landed(rl.at[which, i], r_l.at[4 * which + i])
        for two in range(2):
            first, second = 2 * two, 2 * two + 1

            def column(i):
                return jnp.tile(rl[which, i], (16, 1)).T

            a, b = column(first), column(second)
            top = jnp.maximum(a, b)
            wa, wb = jnp.exp2(a - top), jnp.exp2(b - top)
            value = wa * r[which + 1, first].astype(F32) + wb * r[which + 1, second].astype(F32)
            merged[4 + 2 * which + two] = (value / (wa + wb)).astype(BF)
    for h in range(8):
        band = h - jnp.where(h > f0, 1, 0) - jnp.where(h > f1, 1, 0)
        slot = jnp.where(f0 == h, 6, jnp.where(f1 == h, 7, jnp.clip(band, 0, 5)))
        att[:, h * HD : (h + 1) * HD] = merged[slot]
    landed(wv, w_sem)

    def project(dest):
        for side in range(2):
            for sub in range(2):
                columns = pl.ds(pl.multiple_of(dest * 1024 + side * 512 + sub * 256, 256), 256)
                piece = jnp.dot(att[...], wv[:, columns], preferred_element_type=F32)
                part[dest, side, :, sub * 256 : (sub + 1) * 256] = piece.astype(BF)

    def ship(src, slot, target):
        one = pltpu.make_async_remote_copy(
            src_ref=src,
            dst_ref=got.at[slot],
            send_sem=s_x.at[slot],
            recv_sem=r_x.at[slot],
            device_id=(s, target),
            device_id_type=MESH,
        )
        one.start()
        return one

    across = (hd + 2) % 4
    project(across)
    moved = [ship(part.at[across, 0], 0, right), ship(part.at[across, 1], 1, left)]
    project(right)
    moved.append(ship(part.at[right, 1], 2, right))
    project(left)
    moved.append(ship(part.at[left, 0], 3, left))
    landed(got.at[0], r_x.at[0])
    tmp[0] = (got[0].astype(F32) + part[right, 0].astype(F32)).astype(BF)
    moved.append(ship(tmp.at[0], 4, right))
    landed(got.at[1], r_x.at[1])
    tmp[1] = (got[1].astype(F32) + part[left, 1].astype(F32)).astype(BF)
    moved.append(ship(tmp.at[1], 5, left))
    project(hd)
    for one in sends:
        one.wait_send()
    for j in range(2):
        for h in range(6):
            full_down(h, j).wait_send()
        full_up(j).wait_send()
    for h in range(8):
        when(needed(h), full_sib(h).wait_send)
    for kind in ("a", "b"):
        for d in range(3):
            if d < 2:
                when((z >= d) & (z < 7), band_up(kind, d).wait_send)
            when(z >= d, band_sib(kind, d).wait_send)
    for which in range(3):
        for t in range(4):
            for back in backs(which, t):
                back.wait_send()
    landed(got.at[2], r_x.at[2])
    landed(got.at[3], r_x.at[3])
    landed(got.at[4], r_x.at[4])
    out[:, :512] = (part[hd, 0].astype(F32) + got[4].astype(F32) + got[3].astype(F32)).astype(BF)
    landed(got.at[5], r_x.at[5])
    out[:, 512:] = (part[hd, 1].astype(F32) + got[5].astype(F32) + got[2].astype(F32)).astype(BF)
    for one in moved:
        one.wait_send()


def whole(full_ids, spans, queries, keys_in, values_in, w):
    dma = pltpu.SemaphoreType.DMA
    counts = (8, 8, 12, 12, 2, 2, 2, 2, 12, 12, 2, 2, 3, 3, 3, 3, 8, 8, 12, 12, 8, 8, 6, 6)
    smem = pl.BlockSpec(memory_space=pltpu.SMEM)
    return pl.pallas_call(
        whole_body,
        out_shape=jax.ShapeDtypeStruct((ROWS, 1024), BF),
        in_specs=[smem, smem, VM, VM, VM, ANY],
        out_specs=VM,
        scratch_shapes=[
            pltpu.VMEM((8, ROWS, HD), BF),
            pltpu.VMEM((8, 2, ROWS, HD), BF),
            pltpu.VMEM((1024, 4096), BF),
            pltpu.VMEM((17, 4, 2, ROWS, HD), BF),
            pltpu.VMEM((3, 4, ROWS, HD), BF),
            pltpu.VMEM((3, 4, ROWS, HD), BF),
            pltpu.VMEM((2, 4, 8, ROWS), F32),
            pltpu.VMEM((3, 4, ROWS, HD), BF),
            pltpu.VMEM((2, 4, 8, ROWS), F32),
            pltpu.VMEM((8, ROWS, HD), BF),
            pltpu.VMEM((ROWS, 1024), BF),
            pltpu.VMEM((4, 2, ROWS, 512), BF),
            pltpu.VMEM((6, ROWS, 512), BF),
            pltpu.VMEM((2, ROWS, 512), BF),
            pltpu.VMEM((3, 4, ROWS, HD), F32),
            pltpu.VMEM((3, 4, ROWS, HD), F32),
            pltpu.VMEM((3, 4, ROWS, HD), F32),
            pltpu.VMEM((ROWS, 4 * ROWS), jnp.int32),
            dma(()),
        ]
        + [dma((n,)) for n in counts],
        compiler_params=pltpu.CompilerParams(collective_id=0, has_side_effects=True, vmem_limit_bytes=56 << 20),
        name="whole",
    )(full_ids, spans, queries, keys_in, values_in, w)


def on_device(queries, keys_in, values_in, out_weight, spans, full_ids):
    return whole(full_ids, spans, queries, keys_in, values_in, out_weight)


def solution(mesh):
    placed = (P("seq", "head"), P("seq", "head"), P("seq", "head"), P("head", None), P("head"), P("head"))
    return jax.shard_map(on_device, mesh=mesh, in_specs=placed, out_specs=P("seq", "head"), check_vma=False)
```

```python
import functools
import math

import jax
import jax.numpy as jnp
from jax import lax
from jax.experimental import pallas as pl
from jax.experimental.pallas import tpu as pltpu
from jax.sharding import PartitionSpec as P

HD = 128
ROWS = 256
SCALE2 = HD ** (-0.5) * math.log2(math.e)
FILL = -1e30
FLOOR = -5e29
MESH = pl.DeviceIdType.MESH
ANY = pl.BlockSpec(memory_space=pl.ANY)
VM = pl.BlockSpec(memory_space=pltpu.VMEM)
BF = jnp.bfloat16
F32 = jnp.float32


def position():
    s = lax.axis_index("seq")
    return s, s // 8, (s // 2) % 4, s % 2, lax.axis_index("head")


def pick(slot, f0, f1):
    h = slot + (slot >= f0).astype(jnp.int32)
    h = h + (h >= f1).astype(jnp.int32)
    return jnp.where(slot == 6, f0, jnp.where(slot == 7, f1, h))


def greet(targets):
    barrier = pltpu.get_barrier_semaphore()
    for target in targets:
        pl.semaphore_signal(barrier, inc=1, device_id=target, device_id_type=MESH)
    pl.semaphore_wait(barrier, len(targets))


def plane_peers(s, hd):
    base = (s // 8) * 8
    return [(base + (s + r) % 8, hd) for r in range(1, 8)]


class Push:
    def __init__(self, src, dst, ssem, rsem, target, me, hd):
        self.remote = pltpu.make_async_remote_copy(
            src_ref=src, dst_ref=dst, send_sem=ssem, recv_sem=rsem, device_id=(target, hd), device_id_type=MESH
        )
        self.local = pltpu.make_async_copy(src, dst, rsem)
        self.away = target != me

    def start(self):
        @pl.when(self.away)
        def _():
            self.remote.start()

        @pl.when(jnp.logical_not(self.away))
        def _():
            self.local.start()

    def wait_send(self):
        @pl.when(self.away)
        def _():
            self.remote.wait_send()


def landed(ref, sem):
    pltpu.make_async_copy(ref, ref, sem).wait()


TASKS = (
    (0, 0, 0),
    (0, 0, 1),
    (2, 0, 0),
    (2, 7, 0),
    (2, 1, 0),
    (0, 1, 0),
    (2, 2, 0),
    (0, 1, 1),
    (1, 0, 0),
    (2, 3, 0),
    (2, 4, 0),
    (2, 5, 0),
    (0, 2, 0),
    (0, 2, 1),
    (2, 6, 0),
    (1, 1, 0),
    (1, 2, 0),
)
MOVES = {2: (("f", 7),), 4: (("a", 1),), 6: (("b", 0),), 11: (("b", 1),), 12: (("a", 2),), 16: (("b", 2),)}
DONE = {14: 0, 15: 2}
EARLY = 16


def table(n, values):
    out = jnp.int32(values[0])
    for i, value in enumerate(values[1:], 1):
        out = jnp.where(n == i, value, out)
    return out


def whole_body(
    ids, spans, queries, keys_in, values_in, w, out,
    qh, kvh, wv, kv, qb, o, lse, r, rl, merged, att, part, got, tmp, ab, w_out, w_in, m_sc, l_sc, acc_sc, rel,
    w_sem, s_in, r_in, s_q, r_q, s_fa, r_fa, s_fb, r_fb, s_ff, r_ff, s_fu, r_fu, s_sa, r_sa, s_sb, r_sb, s_sf, r_sf,
    s_o, r_o, s_l, r_l, s_x, r_x, s_w, r_w, s_b, r_b,
):
    s, z, y, c, hd = position()
    pair, par = y // 2, y % 2
    base = z * 8
    up, down = (s + 8) % 64, (s + 56) % 64
    sib = base + 2 * y + (1 - c)
    right, left, across = (hd + 1) % 4, (hd + 3) % 4, (hd + 2) % 4
    half = y // 2
    pltpu.make_async_copy(w, wv, w_sem).start()
    f0, f1 = ids[0] - hd * 8, ids[1] - hd * 8

    def column_of(ref, slot):
        h = pick(jnp.int32(slot), f0, f1)
        first, last = (slot, slot + 2) if slot < 6 else (slot - 6, slot)
        out = ref[:, last * HD : (last + 1) * HD]
        for i in range(first, last):
            out = jnp.where(h == i, ref[:, i * HD : (i + 1) * HD], out)
        return out

    def arrange_kv(slots):
        for i in slots:
            kvh[i, 0] = column_of(keys_in, i)
            kvh[i, 1] = column_of(values_in, i)

    def arrange_q(slots):
        for i in slots:
            qh[i] = column_of(queries, i)

    arrange_kv((6, 7))
    greet(plane_peers(s, hd) + [(up, hd), (down, hd), (s, right), (s, left), (s, across)])

    sends = []

    def push(src, dst, ssem, rsem, target):
        one = Push(src, dst, ssem, rsem, target, s, hd)
        one.start()
        sends.append(one)

    def push_q(i, slot):
        for t in range(4):
            push(qh.at[slot(t)], qb.at[i, place], s_q.at[4 * i + t], r_q.at[4 * i + place], base + 2 * t + half)

    place = 2 * (y % 2) + c
    def prepare():
        row = lax.broadcasted_iota(jnp.int32, (ROWS, 4 * ROWS), 0)
        col = lax.broadcasted_iota(jnp.int32, (ROWS, 4 * ROWS), 1)
        rel[...] = row - col - (col // ROWS) * ROWS
        m_sc[...] = jnp.full_like(m_sc, FLOOR)
        l_sc[...] = jnp.zeros_like(l_sc)
        acc_sc[...] = jnp.zeros_like(acc_sc)

    def hop(src, dst, ssem, rsem, target):
        return pltpu.make_async_remote_copy(
            src_ref=src, dst_ref=dst, send_sem=ssem, recv_sem=rsem, device_id=(target, hd), device_id_type=MESH
        )

    def when(cond, action):
        pl.when(cond)(action)

    mine2 = pl.ds(2 * c, 2)
    other2 = pl.ds(2 * (1 - c), 2)

    def full_down(h, j):
        ref = kv.at[9 + (z + h) % 8, 2 * c + j]
        return hop(ref, ref, s_ff.at[2 * h + j], r_ff.at[2 * h + j], down)

    def full_sib(h):
        ref = kv.at[9 + (z + h) % 8, mine2]
        return hop(ref, ref, s_sf.at[h], r_sf.at[h], sib)

    def needed(h):
        return (z + h) % 8 <= z

    def full_up(j):
        ref = kv.at[9 + z, 2 * c + j]
        return hop(ref, ref, s_fu.at[j], r_fu.at[j], up)

    def move_full(h, j):
        ref = kv.at[9 + (z + h) % 8, 2 * c + j]
        landed(ref, r_in.at[j] if h == 0 else r_fu.at[j] if h == 7 else r_ff.at[2 * h - 2 + j])
        if h < 6:
            full_down(h, j).start()
        if h == 0:
            full_up(j).start()
        if j == 1:
            when(needed(h), full_sib(h).start)

    def band_up(kind, d):
        if kind == "a":
            return hop(kv.at[2 * d + c], kv.at[2 * d + 2 + c], s_fa.at[d], r_fa.at[d], up)
        return hop(kv.at[6 + d, mine2], kv.at[7 + d, mine2], s_fb.at[d], r_fb.at[d], up)

    def band_sib(kind, d):
        if kind == "a":
            return hop(kv.at[2 * d + c], kv.at[2 * d + c], s_sa.at[d], r_sa.at[d], sib)
        return hop(kv.at[6 + d, mine2], kv.at[6 + d, mine2], s_sb.at[d], r_sb.at[d], sib)

    def move_band(kind, d):
        if d == 0 and kind == "a":
            for j in range(4):
                landed(kv.at[c, j], r_in.at[2 + j])
        elif d == 0:
            for j in range(2):
                landed(kv.at[6, 2 * c + j], r_in.at[6 + j])
        else:

            @pl.when(z >= d)
            def _():
                if kind == "a":
                    landed(kv.at[2 * d + c], r_fa.at[d - 1])
                else:
                    landed(kv.at[6 + d, mine2], r_fb.at[d - 1])

        if d < 2:
            when((z >= d) & (z < 7), band_up(kind, d).start)
        when(z >= d, band_sib(kind, d).start)

    for g in range(2):
        push(kvh.at[6 + g], kv.at[9 + z, y], s_in.at[g], r_in.at[y % 2], base + 2 * (2 * g + c) + half)
    arrange_kv(range(4))
    arrange_q(range(4))
    move_full(0, 0)
    move_full(0, 1)
    for t in range(4):
        push(kvh.at[t], kv.at[c, y], s_in.at[2 + t], r_in.at[2 + y], base + 2 * t + c)
    push_q(0, lambda t: t)
    arrange_kv((4, 5))
    arrange_q(range(4, 8))
    prepare()
    move_full(1, 0)
    move_band("a", 0)
    push_q(2, lambda t: 6 + t // 2)
    for g in range(2):
        push(kvh.at[4 + g], kv.at[6, y], s_in.at[6 + g], r_in.at[6 + y % 2], base + 2 * (2 * g + c) + half)
    move_full(1, 1)
    move_full(2, 0)
    push_q(1, lambda t: 4 + t // 2)

    def round_head(src, dst, ssem, rsem):
        return [
            pltpu.make_async_remote_copy(
                src_ref=src(group),
                dst_ref=dst,
                send_sem=ssem.at[i],
                recv_sem=rsem.at[i],
                device_id=(s, group),
                device_id_type=MESH,
            )
            for i, group in enumerate((right, left, across))
        ]

    def arrived(ref, rsem):
        for i, group in enumerate((left, right, across)):
            landed(ref.at[group], rsem.at[i])

    def weights_out():
        return round_head(lambda group: w_out.at[group], w_in.at[hd], s_w, r_w)

    def rows_out():
        return round_head(lambda group: ab.at[hd], ab.at[hd], s_b, r_b)

    landed(wv, w_sem)
    for two in range(2):
        h = jnp.clip(pick(jnp.int32(4 + two), f0, f1), 0, 7)
        for group in range(4):
            w_out[group, two * HD : (two + 1) * HD] = wv[h, :, group * 1024 : (group + 1) * 1024]
    w_in[hd] = w_out[hd]
    for copy in weights_out():
        copy.start()

    reach_a = spans[jnp.clip(pick(y, f0, f1), 0, 7)]
    reach_b = spans[jnp.clip(pick(4 + pair, f0, f1), 0, 7)]
    q_start = base * ROWS + c * 4 * ROWS

    def absorb(which, chunk, first, units, off, reach, masked):
        keys = units * ROWS
        k = kv[chunk, pl.ds(first, units), 0].reshape(keys, HD)
        v = kv[chunk, pl.ds(first, units), 1].reshape(keys, HD)

        def scores(t):
            sc = SCALE2 * lax.dot_general(
                qb[which, t], k, (((1,), (1,)), ((), ())), preferred_element_type=F32
            )
            if masked:
                at = rel[:, :keys]
                low = -(off + t * ROWS)
                sc = jnp.where((at >= low) & (at < low + reach), sc, FILL)
            return sc

        def soft(t, sc):
            m_old = m_sc[which, t]
            m_new = jnp.maximum(m_old, jnp.max(sc, axis=1, keepdims=True))
            alpha = jnp.exp2(m_old - m_new)
            p = jnp.exp2(sc - jnp.tile(m_new, (1, keys // HD)))
            m_sc[which, t] = m_new
            l_sc[which, t] = alpha * l_sc[which, t] + jnp.sum(p, axis=1, keepdims=True)
            return p.astype(BF), alpha

        def gather(t, p, alpha):
            acc_sc[which, t] = alpha * acc_sc[which, t] + jnp.dot(p, v, preferred_element_type=F32)

        current, pending = scores(0), None
        for t in range(4):
            following = scores(t + 1) if t < 3 else None
            weights = soft(t, current)
            if pending is not None:
                gather(*pending)
            pending = (t, *weights)
            current = following
        gather(*pending)

    def step(n, _):
        for unit in range(5, 14):

            @pl.when(n == unit - 4)
            def _(unit=unit):
                move_full(unit // 2, unit % 2)

        @pl.when(n == EARLY)
        def _():
            sum_early()

        for at, moves in MOVES.items():

            @pl.when(n == at)
            def _(moves=moves):
                for kind, d in moves:
                    if kind == "f":
                        move_full(d, 0)
                        move_full(d, 1)
                    else:
                        move_band(kind, d)

        for at, which in DONE.items():

            @pl.when(n == at)
            def _(which=which):
                send_back(which)

        for at, (which, d, other) in enumerate(TASKS):

            @pl.when(n == at)
            def _(which=which, d=d, other=other):
                if d == 0 and not other:
                    for j in range(4):
                        landed(qb.at[which, j], r_q.at[4 * which + j])
                if which == 0 and other:
                    when(z >= d, lambda: landed(kv.at[2 * d + 1 - c], r_sa.at[d]))
                if which == 1:
                    when(z >= d, lambda: landed(kv.at[6 + d, other2], r_sb.at[d]))
                if which == 2:
                    when(needed(d), lambda: landed(kv.at[9 + (z + d) % 8, other2], r_sf.at[d]))

        which = table(n, [t[0] for t in TASKS])
        d = table(n, [t[1] for t in TASKS])
        other = table(n, [t[2] for t in TASKS])
        side = jnp.where(other == 1, 1 - c, c)
        full = which == 2
        plane = jnp.where(full, (z + d) % 8, z - d)
        chunk = jnp.where(full, 9 + plane, jnp.where(which == 1, 6 + d, 2 * d + side))
        valid = jnp.where(full, plane <= z, z >= d)
        parity = jnp.where(which == 0, side, par)
        off = q_start - plane * 8 * ROWS - parity * ROWS
        reach = jnp.where(full, 1 << 20, jnp.where(which == 1, reach_b, reach_a))
        lower = (d == 0) & (c == 0)
        upper = jnp.logical_not(full) & (d == 2) & (c == 1)
        plain = full & (d > 0)

        @pl.when(valid & plain)
        def _():
            absorb(which, chunk, 0, 4, off, reach, False)

        @pl.when(valid & jnp.logical_not(plain | lower | upper))
        def _():
            absorb(which, chunk, 0, 4, off, reach, True)

        @pl.when(valid & (lower | upper))
        def _():
            first = jnp.where(upper, 2, 0)
            absorb(which, chunk, first, 2, off - first * 2 * ROWS, reach, True)

        return 0

    def backs(which, t):
        home = base + 2 * (2 * c + t // 2) + t % 2
        i = 4 * which
        out = [Push(o.at[which, t], r.at[which, y], s_o.at[i + t], r_o.at[i + y], home, s, hd)]
        if which:
            i -= 4
            out.append(Push(lse.at[which - 1, t], rl.at[which - 1, y], s_l.at[i + t], r_l.at[i + y], home, s, hd))
        return out

    def send_back(which):
        def one(t, _):
            total = l_sc[which, t]
            safe = jnp.where(total > 0.0, total, 1.0)
            o[which, t] = (acc_sc[which, t] / safe).astype(BF)
            if which:
                level = jnp.where(total > 0.0, m_sc[which, t] + jnp.log2(safe), FILL)
                lse[which - 1, t] = level.T[:8]
            for back in backs(which, t):
                back.start()
            return 0

        lax.fori_loop(0, 4, one, 0)

    def merge(which, two):
        def column(i):
            return jnp.tile(rl[which - 1, i], (16, 1)).T

        first, second = 2 * two, 2 * two + 1
        a, b = column(first), column(second)
        top = jnp.maximum(a, b)
        wa, wb = jnp.exp2(a - top), jnp.exp2(b - top)
        value = wa * r[which, first].astype(F32) + wb * r[which, second].astype(F32)
        return (value / (wa + wb)).astype(BF)

    def rows_landed(which):
        for i in range(4):
            landed(r.at[which, i], r_o.at[4 * which + i])
            if which:
                landed(rl.at[which - 1, i], r_l.at[4 * which - 4 + i])

    def project(dest):
        for side in range(2):
            for sub in range(2):
                columns = pl.ds(pl.multiple_of(dest * 1024 + side * 512 + sub * 256, 256), 256)
                piece = jnp.dot(att[...], wv[:, :, columns].reshape(1024, 256), preferred_element_type=F32)
                part[dest, side, :, sub * 256 : (sub + 1) * 256] = piece.astype(BF)

    def ship(slot):
        src, target = (
            (lambda: part.at[across, 0], right),
            (lambda: part.at[across, 1], left),
            (lambda: part.at[right, 1], right),
            (lambda: part.at[left, 0], left),
            (lambda: tmp.at[0], right),
            (lambda: tmp.at[1], left),
        )[slot]
        return pltpu.make_async_remote_copy(
            src_ref=src(),
            dst_ref=got.at[slot],
            send_sem=s_x.at[slot],
            recv_sem=r_x.at[slot],
            device_id=(s, target),
            device_id_type=MESH,
        )

    def sum_early():
        rows_landed(0)
        for i in range(4):
            merged[i] = r[0, i]
        merged[4:6] = jnp.zeros((2, ROWS, HD), BF)
        rows_landed(2)
        for two in range(2):
            merged[6 + two] = merge(2, two)
        for h in range(8):
            band = h - jnp.where(h > f0, 1, 0) - jnp.where(h > f1, 1, 0)
            slot = jnp.where(f0 == h, 6, jnp.where(f1 == h, 7, jnp.clip(band, 0, 5)))
            att[:, h * HD : (h + 1) * HD] = merged[slot]
        project(across)
        ship(0).start()
        ship(1).start()
        project(right)
        ship(2).start()
        project(left)
        ship(3).start()

    lax.fori_loop(0, len(TASKS), step, 0)
    send_back(1)
    landed(got.at[0], r_x.at[0])
    tmp[0] = (got[0].astype(F32) + part[right, 0].astype(F32)).astype(BF)
    ship(4).start()
    landed(got.at[1], r_x.at[1])
    tmp[1] = (got[1].astype(F32) + part[left, 1].astype(F32)).astype(BF)
    ship(5).start()
    project(hd)
    rows_landed(1)
    for two in range(2):
        ab[hd, :, two * HD : (two + 1) * HD] = merge(1, two)
    for copy in rows_out():
        copy.start()
    for one in sends:
        one.wait_send()
    for j in range(2):
        for h in range(6):
            full_down(h, j).wait_send()
        full_up(j).wait_send()
    for h in range(8):
        when(needed(h), full_sib(h).wait_send)
    for kind in ("a", "b"):
        for d in range(3):
            if d < 2:
                when((z >= d) & (z < 7), band_up(kind, d).wait_send)
            when(z >= d, band_sib(kind, d).wait_send)
    for which in range(3):
        for t in range(4):
            for back in backs(which, t):
                back.wait_send()
    for copy in weights_out():
        copy.wait_send()
    arrived(w_in, r_w)
    for i in range(2, 6):
        landed(got.at[i], r_x.at[i])
    arrived(ab, r_b)
    for side in range(2):
        total = part[hd, side].astype(F32) + got[4 + side].astype(F32) + got[3 - side].astype(F32)
        for group in range(4):
            total = total + jnp.dot(
                ab[group], w_in[group, :, side * 512 : (side + 1) * 512], preferred_element_type=F32
            )
        out[:, side * 512 : (side + 1) * 512] = total.astype(BF)
    for copy in rows_out():
        copy.wait_send()
    for i in range(6):
        ship(i).wait_send()


def whole(full_ids, spans, queries, keys_in, values_in, w):
    dma = pltpu.SemaphoreType.DMA
    counts = (8, 8, 12, 12, 2, 2, 2, 2, 12, 12, 2, 2, 3, 3, 3, 3, 8, 8, 12, 12, 8, 8, 6, 6, 3, 3, 3, 3)
    smem = pl.BlockSpec(memory_space=pltpu.SMEM)
    return pl.pallas_call(
        whole_body,
        out_shape=jax.ShapeDtypeStruct((ROWS, 1024), BF),
        in_specs=[smem, smem, VM, VM, VM, ANY],
        out_specs=VM,
        scratch_shapes=[
            pltpu.VMEM((8, ROWS, HD), BF),
            pltpu.VMEM((8, 2, ROWS, HD), BF),
            pltpu.VMEM((8, HD, 4096), BF),
            pltpu.VMEM((17, 4, 2, ROWS, HD), BF),
            pltpu.VMEM((3, 4, ROWS, HD), BF),
            pltpu.VMEM((3, 4, ROWS, HD), BF),
            pltpu.VMEM((2, 4, 8, ROWS), F32),
            pltpu.VMEM((3, 4, ROWS, HD), BF),
            pltpu.VMEM((2, 4, 8, ROWS), F32),
            pltpu.VMEM((8, ROWS, HD), BF),
            pltpu.VMEM((ROWS, 1024), BF),
            pltpu.VMEM((4, 2, ROWS, 512), BF),
            pltpu.VMEM((6, ROWS, 512), BF),
            pltpu.VMEM((2, ROWS, 512), BF),
            pltpu.VMEM((4, ROWS, 2 * HD), BF),
            pltpu.VMEM((4, 2 * HD, 1024), BF),
            pltpu.VMEM((4, 2 * HD, 1024), BF),
            pltpu.VMEM((3, 4, ROWS, HD), F32),
            pltpu.VMEM((3, 4, ROWS, HD), F32),
            pltpu.VMEM((3, 4, ROWS, HD), F32),
            pltpu.VMEM((ROWS, 4 * ROWS), jnp.int32),
            dma(()),
        ]
        + [dma((n,)) for n in counts],
        compiler_params=pltpu.CompilerParams(collective_id=0, has_side_effects=True, vmem_limit_bytes=56 << 20),
        name="whole",
    )(full_ids, spans, queries, keys_in, values_in, w)


def on_device(queries, keys_in, values_in, out_weight, spans, full_ids):
    return whole(full_ids, spans, queries, keys_in, values_in, out_weight.reshape(8, HD, 4096))


def solution(mesh):
    placed = (P("seq", "head"), P("seq", "head"), P("seq", "head"), P("head", None), P("head"), P("head"))
    return jax.shard_map(on_device, mesh=mesh, in_specs=placed, out_specs=P("seq", "head"), check_vma=False)
```

```python
import functools
import math

import jax
import jax.numpy as jnp
from jax import lax
from jax.experimental import pallas as pl
from jax.experimental.pallas import tpu as pltpu
from jax.sharding import PartitionSpec as P

HD = 128
ROWS = 256
SCALE2 = HD ** (-0.5) * math.log2(math.e)
FILL = -1e30
FLOOR = -5e29
MESH = pl.DeviceIdType.MESH
ANY = pl.BlockSpec(memory_space=pl.ANY)
VM = pl.BlockSpec(memory_space=pltpu.VMEM)
BF = jnp.bfloat16
F32 = jnp.float32


def position():
    s = lax.axis_index("seq")
    return s, s // 8, (s // 2) % 4, s % 2, lax.axis_index("head")


def pick(slot, f0, f1):
    h = slot + (slot >= f0).astype(jnp.int32)
    h = h + (h >= f1).astype(jnp.int32)
    return jnp.where(slot == 6, f0, jnp.where(slot == 7, f1, h))


def greet(targets):
    barrier = pltpu.get_barrier_semaphore()
    for target in targets:
        pl.semaphore_signal(barrier, inc=1, device_id=target, device_id_type=MESH)
    pl.semaphore_wait(barrier, len(targets))


def plane_peers(s, hd):
    base = (s // 8) * 8
    return [(base + (s + r) % 8, hd) for r in range(1, 8)]


class Push:
    def __init__(self, src, dst, ssem, rsem, target, me, hd):
        self.remote = pltpu.make_async_remote_copy(
            src_ref=src, dst_ref=dst, send_sem=ssem, recv_sem=rsem, device_id=(target, hd), device_id_type=MESH
        )
        self.local = pltpu.make_async_copy(src, dst, rsem)
        self.away = target != me

    def start(self):
        @pl.when(self.away)
        def _():
            self.remote.start()

        @pl.when(jnp.logical_not(self.away))
        def _():
            self.local.start()

    def wait_send(self):
        @pl.when(self.away)
        def _():
            self.remote.wait_send()


def landed(ref, sem):
    pltpu.make_async_copy(ref, ref, sem).wait()


TASKS = (
    (0, 0, 0),
    (0, 0, 1),
    (2, 0, 0),
    (2, 7, 0),
    (1, 0, 0),
    (2, 1, 0),
    (0, 1, 0),
    (2, 2, 0),
    (0, 1, 1),
    (2, 3, 0),
    (1, 1, 0),
    (2, 4, 0),
    (2, 5, 0),
    (0, 2, 0),
    (2, 6, 0),
    (0, 2, 1),
    (1, 2, 0),
)
MOVES = {2: (("f", 7),), 3: (("b", 0),), 4: (("a", 1),), 8: (("b", 1),), 12: (("a", 2),), 15: (("b", 2),)}
DONE = {15: 2, 16: 0}


def table(n, values):
    out = jnp.int32(values[0])
    for i, value in enumerate(values[1:], 1):
        out = jnp.where(n == i, value, out)
    return out


def whole_body(
    ids, spans, queries, keys_in, values_in, w, out,
    qh, kvh, wv, kv, qb, o, lse, r, rl, merged, att, part, got, tmp, m_sc, l_sc, acc_sc, rel,
    w_sem, s_in, r_in, s_q, r_q, s_fa, r_fa, s_fb, r_fb, s_ff, r_ff, s_fu, r_fu, s_sa, r_sa, s_sb, r_sb, s_sf, r_sf,
    s_o, r_o, s_l, r_l, s_x, r_x,
):
    s, z, y, c, hd = position()
    pair, par = y // 2, y % 2
    base = z * 8
    up, down = (s + 8) % 64, (s + 56) % 64
    sib = base + 2 * y + (1 - c)
    right, left = (hd + 1) % 4, (hd + 3) % 4
    half = y // 2
    pltpu.make_async_copy(w, wv, w_sem).start()
    f0, f1 = ids[0] - hd * 8, ids[1] - hd * 8

    def column_of(ref, slot):
        h = pick(jnp.int32(slot), f0, f1)
        first, last = (slot, slot + 2) if slot < 6 else (slot - 6, slot)
        out = ref[:, last * HD : (last + 1) * HD]
        for i in range(first, last):
            out = jnp.where(h == i, ref[:, i * HD : (i + 1) * HD], out)
        return out

    def arrange_kv(slots):
        for i in slots:
            kvh[i, 0] = column_of(keys_in, i)
            kvh[i, 1] = column_of(values_in, i)

    def arrange_q(slots):
        for i in slots:
            qh[i] = column_of(queries, i)

    arrange_kv((6, 7))
    greet(plane_peers(s, hd) + [(up, hd), (down, hd), (s, right), (s, left)])

    sends = []

    def push(src, dst, ssem, rsem, target):
        one = Push(src, dst, ssem, rsem, target, s, hd)
        one.start()
        sends.append(one)

    def push_q(i, slot):
        for t in range(4):
            push(qh.at[slot(t)], qb.at[i, place], s_q.at[4 * i + t], r_q.at[4 * i + place], base + 2 * t + half)

    place = 2 * (y % 2) + c
    def prepare():
        row = lax.broadcasted_iota(jnp.int32, (ROWS, 4 * ROWS), 0)
        col = lax.broadcasted_iota(jnp.int32, (ROWS, 4 * ROWS), 1)
        rel[...] = row - col - (col // ROWS) * ROWS
        m_sc[...] = jnp.full_like(m_sc, FLOOR)
        l_sc[...] = jnp.zeros_like(l_sc)
        acc_sc[...] = jnp.zeros_like(acc_sc)

    def hop(src, dst, ssem, rsem, target):
        return pltpu.make_async_remote_copy(
            src_ref=src, dst_ref=dst, send_sem=ssem, recv_sem=rsem, device_id=(target, hd), device_id_type=MESH
        )

    def when(cond, action):
        pl.when(cond)(action)

    mine2 = pl.ds(2 * c, 2)
    other2 = pl.ds(2 * (1 - c), 2)

    def full_down(h, j):
        ref = kv.at[9 + (z + h) % 8, 2 * c + j]
        return hop(ref, ref, s_ff.at[2 * h + j], r_ff.at[2 * h + j], down)

    def full_sib(h):
        ref = kv.at[9 + (z + h) % 8, mine2]
        return hop(ref, ref, s_sf.at[h], r_sf.at[h], sib)

    def needed(h):
        return (z + h) % 8 <= z

    def full_up(j):
        ref = kv.at[9 + z, 2 * c + j]
        return hop(ref, ref, s_fu.at[j], r_fu.at[j], up)

    def move_full(h, j):
        ref = kv.at[9 + (z + h) % 8, 2 * c + j]
        landed(ref, r_in.at[j] if h == 0 else r_fu.at[j] if h == 7 else r_ff.at[2 * h - 2 + j])
        if h < 6:
            full_down(h, j).start()
        if h == 0:
            full_up(j).start()
        if j == 1:
            when(needed(h), full_sib(h).start)

    def band_up(kind, d):
        if kind == "a":
            return hop(kv.at[2 * d + c], kv.at[2 * d + 2 + c], s_fa.at[d], r_fa.at[d], up)
        return hop(kv.at[6 + d, mine2], kv.at[7 + d, mine2], s_fb.at[d], r_fb.at[d], up)

    def band_sib(kind, d):
        if kind == "a":
            return hop(kv.at[2 * d + c], kv.at[2 * d + c], s_sa.at[d], r_sa.at[d], sib)
        return hop(kv.at[6 + d, mine2], kv.at[6 + d, mine2], s_sb.at[d], r_sb.at[d], sib)

    def move_band(kind, d):
        if d == 0 and kind == "a":
            for j in range(4):
                landed(kv.at[c, j], r_in.at[2 + j])
        elif d == 0:
            for j in range(2):
                landed(kv.at[6, 2 * c + j], r_in.at[6 + j])
        else:

            @pl.when(z >= d)
            def _():
                if kind == "a":
                    landed(kv.at[2 * d + c], r_fa.at[d - 1])
                else:
                    landed(kv.at[6 + d, mine2], r_fb.at[d - 1])

        if d < 2:
            when((z >= d) & (z < 7), band_up(kind, d).start)
        when(z >= d, band_sib(kind, d).start)

    for g in range(2):
        push(kvh.at[6 + g], kv.at[9 + z, y], s_in.at[g], r_in.at[y % 2], base + 2 * (2 * g + c) + half)
    arrange_kv(range(4))
    arrange_q(range(4))
    move_full(0, 0)
    move_full(0, 1)
    for t in range(4):
        push(kvh.at[t], kv.at[c, y], s_in.at[2 + t], r_in.at[2 + y], base + 2 * t + c)
    push_q(0, lambda t: t)
    arrange_kv((4, 5))
    arrange_q(range(4, 8))
    prepare()
    move_full(1, 0)
    move_band("a", 0)
    push_q(2, lambda t: 6 + t // 2)
    for g in range(2):
        push(kvh.at[4 + g], kv.at[6, y], s_in.at[6 + g], r_in.at[6 + y % 2], base + 2 * (2 * g + c) + half)
    move_full(1, 1)
    move_full(2, 0)
    push_q(1, lambda t: 4 + t // 2)

    reach_a = spans[jnp.clip(pick(y, f0, f1), 0, 7)]
    reach_b = spans[jnp.clip(pick(4 + pair, f0, f1), 0, 7)]
    q_start = base * ROWS + c * 4 * ROWS

    def absorb(which, chunk, first, units, off, reach, masked):
        keys = units * ROWS
        k = kv[chunk, pl.ds(first, units), 0].reshape(keys, HD)
        v = kv[chunk, pl.ds(first, units), 1].reshape(keys, HD)

        def scores(t):
            sc = SCALE2 * lax.dot_general(
                qb[which, t], k, (((1,), (1,)), ((), ())), preferred_element_type=F32
            )
            if masked:
                at = rel[:, :keys]
                low = -(off + t * ROWS)
                seen = at < low + reach
                if masked == 2:
                    seen = seen & (at >= low)
                sc = jnp.where(seen, sc, FILL)
            return sc

        def soft(t, sc):
            m_old = m_sc[which, t]
            m_new = jnp.maximum(m_old, jnp.max(sc, axis=1, keepdims=True))
            alpha = jnp.exp2(m_old - m_new)
            p = jnp.exp2(sc - jnp.tile(m_new, (1, keys // HD)))
            m_sc[which, t] = m_new
            l_sc[which, t] = alpha * l_sc[which, t] + jnp.sum(p, axis=1, keepdims=True)
            return p.astype(BF), alpha

        def gather(t, p, alpha):
            acc_sc[which, t] = alpha * acc_sc[which, t] + jnp.dot(p, v, preferred_element_type=F32)

        current, pending = scores(0), None
        for t in range(4):
            following = scores(t + 1) if t < 3 else None
            weights = soft(t, current)
            if pending is not None:
                gather(*pending)
            pending = (t, *weights)
            current = following
        gather(*pending)

    def step(n, _):
        for unit in range(5, 14):

            @pl.when(n == unit - 4)
            def _(unit=unit):
                move_full(unit // 2, unit % 2)

        for at, moves in MOVES.items():

            @pl.when(n == at)
            def _(moves=moves):
                for kind, d in moves:
                    if kind == "f":
                        move_full(d, 0)
                        move_full(d, 1)
                    else:
                        move_band(kind, d)

        for at, which in DONE.items():

            @pl.when(n == at)
            def _(which=which):
                send_back(which)

        for at, (which, d, other) in enumerate(TASKS):

            @pl.when(n == at)
            def _(which=which, d=d, other=other):
                if d == 0 and not other:
                    for j in range(4):
                        landed(qb.at[which, j], r_q.at[4 * which + j])
                if which == 0 and other:
                    when(z >= d, lambda: landed(kv.at[2 * d + 1 - c], r_sa.at[d]))
                if which == 1:
                    when(z >= d, lambda: landed(kv.at[6 + d, other2], r_sb.at[d]))
                if which == 2:
                    when(needed(d), lambda: landed(kv.at[9 + (z + d) % 8, other2], r_sf.at[d]))

        which = table(n, [t[0] for t in TASKS])
        d = table(n, [t[1] for t in TASKS])
        other = table(n, [t[2] for t in TASKS])
        side = jnp.where(other == 1, 1 - c, c)
        full = which == 2
        plane = jnp.where(full, (z + d) % 8, z - d)
        chunk = jnp.where(full, 9 + plane, jnp.where(which == 1, 6 + d, 2 * d + side))
        valid = jnp.where(full, plane <= z, z >= d)
        parity = jnp.where(which == 0, side, par)
        off = q_start - plane * 8 * ROWS - parity * ROWS
        reach = jnp.where(full, 1 << 20, jnp.where(which == 1, reach_b, reach_a))
        lower = (d == 0) & (c == 0)
        upper = jnp.logical_not(full) & (d == 2) & (c == 1)
        plain = full & (d > 0)

        @pl.when(valid & plain)
        def _():
            absorb(which, chunk, 0, 4, off, reach, 0)

        @pl.when(valid & (d == 0) & jnp.logical_not(lower))
        def _():
            absorb(which, chunk, 0, 4, off, reach, 2)

        @pl.when(valid & (d > 0) & jnp.logical_not(plain | upper))
        def _():
            absorb(which, chunk, 0, 4, off, reach, 1)

        @pl.when(valid & (lower | upper))
        def _():
            first = jnp.where(upper, 2, 0)
            absorb(which, chunk, first, 2, off - first * 2 * ROWS, reach, 2)

        return 0

    def backs(which, t):
        home = base + 2 * (2 * c + t // 2) + t % 2
        i = 4 * which
        out = [Push(o.at[which, t], r.at[which, y], s_o.at[i + t], r_o.at[i + y], home, s, hd)]
        if which:
            i -= 4
            out.append(Push(lse.at[which - 1, t], rl.at[which - 1, y], s_l.at[i + t], r_l.at[i + y], home, s, hd))
        return out

    def send_back(which):
        def one(t, _):
            total = l_sc[which, t]
            safe = jnp.where(total > 0.0, total, 1.0)
            o[which, t] = (acc_sc[which, t] / safe).astype(BF)
            if which:
                level = jnp.where(total > 0.0, m_sc[which, t] + jnp.log2(safe), FILL)
                lse[which - 1, t] = level.T[:8]
            for back in backs(which, t):
                back.start()
            return 0

        lax.fori_loop(0, 4, one, 0)

    lax.fori_loop(0, len(TASKS), step, 0)
    send_back(1)
    for i in range(4):
        landed(r.at[0, i], r_o.at[i])
        merged[i] = r[0, i]
    for which in (1, 0):
        for i in range(4):
            landed(r.at[which + 1, i], r_o.at[4 * which + 4 + i])
            landed(rl.at[which, i], r_l.at[4 * which + i])
        for two in range(2):
            first, second = 2 * two, 2 * two + 1

            def column(i):
                return jnp.tile(rl[which, i], (16, 1)).T

            a, b = column(first), column(second)
            top = jnp.maximum(a, b)
            wa, wb = jnp.exp2(a - top), jnp.exp2(b - top)
            value = wa * r[which + 1, first].astype(F32) + wb * r[which + 1, second].astype(F32)
            merged[4 + 2 * which + two] = (value / (wa + wb)).astype(BF)
    for h in range(8):
        band = h - jnp.where(h > f0, 1, 0) - jnp.where(h > f1, 1, 0)
        slot = jnp.where(f0 == h, 6, jnp.where(f1 == h, 7, jnp.clip(band, 0, 5)))
        att[:, h * HD : (h + 1) * HD] = merged[slot]
    landed(wv, w_sem)

    def project(dest, sides=(0, 1)):
        for side in sides:
            for sub in range(2):
                columns = pl.ds(pl.multiple_of(dest * 1024 + side * 512 + sub * 256, 256), 256)
                piece = jnp.dot(att[...], wv[:, columns], preferred_element_type=F32)
                part[dest, side, :, sub * 256 : (sub + 1) * 256] = piece.astype(BF)

    def ship(src, slot, target):
        one = pltpu.make_async_remote_copy(
            src_ref=src,
            dst_ref=got.at[slot],
            send_sem=s_x.at[slot],
            recv_sem=r_x.at[slot],
            device_id=(s, target),
            device_id_type=MESH,
        )
        one.start()
        return one

    across = (hd + 2) % 4
    project(across, (0,))
    moved = [ship(part.at[across, 0], 0, right)]
    project(across, (1,))
    moved.append(ship(part.at[across, 1], 1, left))
    project(right)
    moved.append(ship(part.at[right, 1], 2, right))
    project(left)
    moved.append(ship(part.at[left, 0], 3, left))
    landed(got.at[0], r_x.at[0])
    tmp[0] = (got[0].astype(F32) + part[right, 0].astype(F32)).astype(BF)
    moved.append(ship(tmp.at[0], 4, right))
    landed(got.at[1], r_x.at[1])
    tmp[1] = (got[1].astype(F32) + part[left, 1].astype(F32)).astype(BF)
    moved.append(ship(tmp.at[1], 5, left))
    project(hd)
    for one in sends:
        one.wait_send()
    for j in range(2):
        for h in range(6):
            full_down(h, j).wait_send()
        full_up(j).wait_send()
    for h in range(8):
        when(needed(h), full_sib(h).wait_send)
    for kind in ("a", "b"):
        for d in range(3):
            if d < 2:
                when((z >= d) & (z < 7), band_up(kind, d).wait_send)
            when(z >= d, band_sib(kind, d).wait_send)
    for which in range(3):
        for t in range(4):
            for back in backs(which, t):
                back.wait_send()
    landed(got.at[2], r_x.at[2])
    landed(got.at[3], r_x.at[3])
    landed(got.at[4], r_x.at[4])
    out[:, :512] = (part[hd, 0].astype(F32) + got[4].astype(F32) + got[3].astype(F32)).astype(BF)
    landed(got.at[5], r_x.at[5])
    out[:, 512:] = (part[hd, 1].astype(F32) + got[5].astype(F32) + got[2].astype(F32)).astype(BF)
    for one in moved:
        one.wait_send()


def whole(full_ids, spans, queries, keys_in, values_in, w):
    dma = pltpu.SemaphoreType.DMA
    counts = (8, 8, 12, 12, 2, 2, 2, 2, 12, 12, 2, 2, 3, 3, 3, 3, 8, 8, 12, 12, 8, 8, 6, 6)
    smem = pl.BlockSpec(memory_space=pltpu.SMEM)
    return pl.pallas_call(
        whole_body,
        out_shape=jax.ShapeDtypeStruct((ROWS, 1024), BF),
        in_specs=[smem, smem, VM, VM, VM, ANY],
        out_specs=VM,
        scratch_shapes=[
            pltpu.VMEM((8, ROWS, HD), BF),
            pltpu.VMEM((8, 2, ROWS, HD), BF),
            pltpu.VMEM((1024, 4096), BF),
            pltpu.VMEM((17, 4, 2, ROWS, HD), BF),
            pltpu.VMEM((3, 4, ROWS, HD), BF),
            pltpu.VMEM((3, 4, ROWS, HD), BF),
            pltpu.VMEM((2, 4, 8, ROWS), F32),
            pltpu.VMEM((3, 4, ROWS, HD), BF),
            pltpu.VMEM((2, 4, 8, ROWS), F32),
            pltpu.VMEM((8, ROWS, HD), BF),
            pltpu.VMEM((ROWS, 1024), BF),
            pltpu.VMEM((4, 2, ROWS, 512), BF),
            pltpu.VMEM((6, ROWS, 512), BF),
            pltpu.VMEM((2, ROWS, 512), BF),
            pltpu.VMEM((3, 4, ROWS, HD), F32),
            pltpu.VMEM((3, 4, ROWS, HD), F32),
            pltpu.VMEM((3, 4, ROWS, HD), F32),
            pltpu.VMEM((ROWS, 4 * ROWS), jnp.int32),
            dma(()),
        ]
        + [dma((n,)) for n in counts],
        compiler_params=pltpu.CompilerParams(collective_id=0, has_side_effects=True, vmem_limit_bytes=56 << 20),
        name="whole",
    )(full_ids, spans, queries, keys_in, values_in, w)


def on_device(queries, keys_in, values_in, out_weight, spans, full_ids):
    return whole(full_ids, spans, queries, keys_in, values_in, out_weight)


def solution(mesh):
    placed = (P("seq", "head"), P("seq", "head"), P("seq", "head"), P("head", None), P("head"), P("head"))
    return jax.shard_map(on_device, mesh=mesh, in_specs=placed, out_specs=P("seq", "head"), check_vma=False)
```
